32 devices in a mesh: seq: 16 (over z, y, x), dp: 2 (over core).
Axes of the slice: x: 2, y: 2, z: 4, core: 2. Of those that a mesh axis runs over, the one named last changes fastest.
Arguments:
- clip: bfloat16 [16, 128, 1152], P('seq'), may hold values from -40 to 40
- offsets: bfloat16 [2, 16, 128, 1152], P('dp', 'seq'), may hold values from -6 to 6
- cotangent: bfloat16 [2, 16, 128, 1152], P('dp', 'seq'), may hold values from -6 to 6
- gain_time: float32 [1152], replicated, may hold values from 0.1 to 1.9
- gain_space: float32 [1152], replicated, may hold values from 0.1 to 1.9
- proj_time: bfloat16 [1152, 1728], P('dp'), may hold values from -0.1875 to 0.1875
- out_time: bfloat16 [576, 1152], P('dp'), may hold values from -0.25 to 0.25
- proj_space: bfloat16 [1152, 1728], P('dp'), may hold values from -0.1875 to 0.1875
- out_space: bfloat16 [576, 1152], P('dp'), may hold values from -0.25 to 0.25
- bias_time: float32 [8, 16, 16], replicated, may hold values from -3 to 303
- bias_space: float32 [8, 128, 128], P(None, 'dp'), may hold values from -3 to 303
Outputs:
- clip_grad: float32 [16, 128, 1152], P('seq', 'dp')
The draws below stay inside these ranges and needn't reach their ends.
All inputs are finite; a program needn't handle non-finite values.
Results may differ from the reference program's by a relative error of at most 0.015.
Values may be sent and summed in bfloat16 or wider, within the bound.
A program may use at most 64 MiB of HBM per device.

```python
import math
import jax
import jax.numpy as jnp
from jax import lax

D = 1152
HEADS = 8
HD = 72
POS = 128
FRAMES = 16
GROUPS = 2
N_DP = 2


def score_table(key, length):
    base = jax.random.truncated_normal(key, -3.0, 3.0, (HEADS, length, length), jnp.float32)
    return base


def draw_bias_time(key, part):
    return score_table(jax.random.fold_in(key, 101), FRAMES)


def draw_bias_space(key, part):
    return score_table(jax.random.fold_in(key, 202), POS)


def draw_clip(key, part):
    base_key = jax.random.fold_in(key, 303)
    base = jax.random.truncated_normal(base_key, -4.0, 4.0, (FRAMES, POS, D), jnp.float32)
    return base.astype(jnp.bfloat16)


def raised(drawn, stream_key, source, target, parts, factor):
    def block_of(position):
        return (jnp.arange(drawn.shape[position]) // (drawn.shape[position] // parts)).reshape((-1,) + (1,) * (drawn.ndim - 1 - position))

    first = jax.random.permutation(stream_key, parts)[block_of(target)]
    far = (block_of(target) + parts // 2) % parts
    return jnp.where((block_of(source) == first) | (block_of(source) == far), factor * drawn, drawn)


def block_scale(stream_key, dims, split, smallest, high):
    def one(position, blocks):
        heights = jax.random.uniform(jax.random.fold_in(jax.random.fold_in(stream_key, 6), position), (blocks,), jnp.float32, smallest / len(split), high / len(split))
        return jnp.repeat(jnp.exp(heights), dims[position] // blocks).reshape((-1,) + (1,) * (len(dims) - position - 1))

    loudness = one(*split[0])
    for cut in split[1:]:
        loudness = loudness * one(*cut)
    return loudness


def gaussian(stream_key, dims, spread, limit, cuts=(), kind=jnp.bfloat16):
    loudness = block_scale(stream_key, dims, cuts, -0.22, 0.18) if cuts else 1.0
    drawn = jax.random.normal(stream_key, dims, jnp.float32) * spread * loudness
    return jnp.minimum(jnp.maximum(drawn, -limit), limit).astype(kind)


def gaussian_with(own_key, extent, width, bound, split, heavy, held_as=jnp.bfloat16):
    result = width * jax.random.normal(own_key, extent, jnp.float32)
    if split:
        result = result * block_scale(own_key, extent, split, -0.22, 0.18)
    return jnp.clip(raised(result, jax.random.fold_in(own_key, 3), *heavy), -bound, bound).astype(held_as)


def setup_inputs(seed: int = 0) -> dict:
    key_list = jax.random.split(jax.random.key(seed), 12)
    clip = draw_clip(jax.random.fold_in(key_list[11], 71), 0)
    offsets = gaussian(key_list[1], (GROUPS, FRAMES, POS, D), 1.0, 6.0, ((0, 2), (1, 16)))
    cotangent = gaussian_with(key_list[2], (GROUPS, FRAMES, POS, D), 1.0, 6.0, ((0, 2), (1, 16)), (0, 2, 2, 2.0))
    gain_time = jnp.clip(1.0 + 0.18 * jax.random.normal(key_list[3], (D,), jnp.float32), 0.1, 1.9)
    gain_space = jnp.clip(1.0 + 0.18 * jax.random.normal(key_list[4], (D,), jnp.float32), 0.1, 1.9)
    proj_time = gaussian(key_list[5], (D, 3 * HEADS * HD), D ** -0.5, 0.1875, ((0, 2),))
    out_time = gaussian(key_list[6], (HEADS * HD, D), (HEADS * HD) ** -0.5, 0.25, ((0, 2),))
    proj_space = gaussian(key_list[7], (D, 3 * HEADS * HD), D ** -0.5, 0.1875, ((0, 2),))
    out_space = gaussian(key_list[8], (HEADS * HD, D), (HEADS * HD) ** -0.5, 0.25, ((0, 2),))
    bias_time = draw_bias_time(jax.random.fold_in(key_list[11], 71), 0)
    bias_space = draw_bias_space(jax.random.fold_in(key_list[11], 71), 0)
    return dict(clip=clip, offsets=offsets, cotangent=cotangent, gain_time=gain_time, gain_space=gain_space, proj_time=proj_time, out_time=out_time, proj_space=proj_space, out_space=out_space, bias_time=bias_time, bias_space=bias_space)


epsilon = 1e-06

def rms_norm(hidden_in, gain_vec):
    inv_rms = lax.rsqrt(lax.optimization_barrier(jnp.mean(hidden_in * hidden_in, axis=-1, keepdims=True)) + epsilon)
    return ((hidden_in * inv_rms * gain_vec).astype(jnp.bfloat16), inv_rms)

def norm_back(hidden_in, inv_rms, gain_vec, grad_normed):
    weighted = grad_normed.astype(jnp.float32) * gain_vec
    cubed = inv_rms * inv_rms * inv_rms
    return inv_rms * weighted - hidden_in * cubed * lax.optimization_barrier(jnp.mean(weighted * hidden_in, axis=-1, keepdims=True))

def layout_forms(frame_major):
    if frame_major:
        return ('lbhe', 'mbhe')
    return ('blhe', 'bmhe')

def attend(queries, key_rows, values, score_bias, frame_major):
    query_form, key_form = layout_forms(frame_major)
    scaling = 1.0 / math.sqrt(queries.shape[-1])
    scores = jnp.einsum(query_form + ',' + key_form + '->bhlm', queries.astype(jnp.float32), key_rows.astype(jnp.float32)) * scaling + score_bias
    highest = lax.optimization_barrier(jnp.max(scores, axis=-1, keepdims=True))
    exp_scores = jnp.exp(scores - highest)
    probabilities = exp_scores / lax.optimization_barrier(jnp.sum(exp_scores, axis=-1, keepdims=True))
    rounded = probabilities.astype(jnp.bfloat16).astype(jnp.float32)
    context = jnp.einsum('bhlm,' + key_form + '->' + query_form, rounded, values.astype(jnp.float32)).astype(jnp.bfloat16)
    return (context, probabilities)

def attend_back(queries, key_rows, values, probabilities, grad_context, frame_major):
    query_form, key_form = layout_forms(frame_major)
    scaling = 1.0 / math.sqrt(queries.shape[-1])
    rounded = probabilities.astype(jnp.bfloat16).astype(jnp.float32)
    grad_ctx = grad_context.astype(jnp.float32)
    grad_values = jnp.einsum('bhlm,' + query_form + '->' + key_form, rounded, grad_ctx).astype(jnp.bfloat16)
    grad_probs = jnp.einsum(query_form + ',' + key_form + '->bhlm', grad_ctx, values.astype(jnp.float32))
    row_sums = lax.optimization_barrier(jnp.sum(grad_probs * probabilities, axis=-1, keepdims=True))
    grad_scores = (probabilities * (grad_probs - row_sums) * scaling).astype(jnp.bfloat16).astype(jnp.float32)
    grad_queries = jnp.einsum('bhlm,' + key_form + '->' + query_form, grad_scores, key_rows.astype(jnp.float32)).astype(jnp.bfloat16)
    grad_keys = jnp.einsum('bhlm,' + query_form + '->' + key_form, grad_scores, queries.astype(jnp.float32)).astype(jnp.bfloat16)
    return (grad_queries, grad_keys, grad_values)

def times_transposed(left, weight):
    return lax.dot_general(left, weight, (((1,), (1,)), ((), ())), preferred_element_type=jnp.float32)

def reference(clip, offsets, cotangent, gain_time, gain_space, proj_time, out_time, proj_space, out_space, bias_time, bias_space):
    head_cols = HEADS * HD
    grad_total = jnp.zeros((FRAMES, POS, D), jnp.float32)
    for group_idx in range(N_DP):
        hidden_in = clip.astype(jnp.float32) + offsets[group_idx].astype(jnp.float32)
        normed, inv_rms = rms_norm(hidden_in, gain_time)
        stacked = jnp.dot(normed.reshape(-1, D), proj_time, preferred_element_type=jnp.float32).astype(jnp.bfloat16)
        stacked = stacked.reshape(FRAMES, POS, 3, HEADS, HD)
        queries, key_rows, values = (stacked[:, :, 0], stacked[:, :, 1], stacked[:, :, 2])
        context, weights_time = attend(queries, key_rows, values, bias_time, True)
        after_time = hidden_in + jnp.dot(context.reshape(-1, head_cols), out_time, preferred_element_type=jnp.float32).reshape(FRAMES, POS, D)
        normed_space, inv_rms_space = rms_norm(after_time, gain_space)
        stacked_space = jnp.dot(normed_space.reshape(-1, D), proj_space, preferred_element_type=jnp.float32).astype(jnp.bfloat16)
        stacked_space = stacked_space.reshape(FRAMES, POS, 3, HEADS, HD)
        queries_space, keys_space, values_space = (stacked_space[:, :, 0], stacked_space[:, :, 1], stacked_space[:, :, 2])
        unused_context, weights_space = attend(queries_space, keys_space, values_space, bias_space, False)
        grad_out = cotangent[group_idx]
        grad_context = times_transposed(grad_out.reshape(-1, D), out_space).astype(jnp.bfloat16).reshape(FRAMES, POS, HEADS, HD)
        grads_space = attend_back(queries_space, keys_space, values_space, weights_space, grad_context, False)
        grad_normed = times_transposed(jnp.stack(grads_space, axis=2).reshape(-1, 3 * head_cols), proj_space).astype(jnp.bfloat16)
        grad_after = grad_out.astype(jnp.float32) + norm_back(after_time, inv_rms_space, gain_space, grad_normed.reshape(FRAMES, POS, D))
        grad_context_time = times_transposed(grad_after.astype(jnp.bfloat16).reshape(-1, D), out_time).astype(jnp.bfloat16)
        grads_time = attend_back(queries, key_rows, values, weights_time, grad_context_time.reshape(FRAMES, POS, HEADS, HD), True)
        grad_normed_time = times_transposed(jnp.stack(grads_time, axis=2).reshape(-1, 3 * head_cols), proj_time).astype(jnp.bfloat16)
        grad_in = grad_after + norm_back(hidden_in, inv_rms, gain_time, grad_normed_time.reshape(FRAMES, POS, D))
        grad_total = grad_total + grad_in
    return grad_total
```

```python
import functools
import math

import jax
import jax.numpy as jnp
from jax import lax
from jax.experimental import pallas as pl
from jax.experimental.pallas import tpu as pltpu
from jax.sharding import PartitionSpec as P

HEADS = 8
HD = 72


epsilon = 1e-06


def rms_norm(hidden_in, gain_vec):
    inv_rms = lax.rsqrt(jnp.mean(hidden_in * hidden_in, axis=-1, keepdims=True) + epsilon)
    return ((hidden_in * inv_rms * gain_vec).astype(jnp.bfloat16), inv_rms)


def norm_back(hidden_in, inv_rms, gain_vec, grad_normed):
    weighted = grad_normed.astype(jnp.float32) * gain_vec
    cubed = inv_rms * inv_rms * inv_rms
    return inv_rms * weighted - hidden_in * cubed * jnp.mean(
        weighted * hidden_in, axis=-1, keepdims=True
    )


def layout_forms(frame_major):
    if frame_major:
        return ("lbhe", "mbhe")
    return ("blhe", "bmhe")


def attend(queries, key_rows, values, score_bias, frame_major):
    query_form, key_form = layout_forms(frame_major)
    scaling = 1.0 / math.sqrt(queries.shape[-1])
    scores = (
        jnp.einsum(
            query_form + "," + key_form + "->bhlm",
            queries,
            key_rows,
            preferred_element_type=jnp.float32,
        )
        * scaling
        + score_bias
    )
    highest = jnp.max(scores, axis=-1, keepdims=True)
    exp_scores = jnp.exp(scores - highest)
    probabilities = exp_scores / jnp.sum(exp_scores, axis=-1, keepdims=True)
    context = jnp.einsum(
        "bhlm," + key_form + "->" + query_form,
        probabilities.astype(jnp.bfloat16),
        values,
        preferred_element_type=jnp.float32,
    )
    return (context.astype(jnp.bfloat16), probabilities)


def attend_back(queries, key_rows, values, probabilities, grad_context, frame_major):
    query_form, key_form = layout_forms(frame_major)
    scaling = 1.0 / math.sqrt(queries.shape[-1])
    rounded = probabilities.astype(jnp.bfloat16)
    grad_values = jnp.einsum(
        "bhlm," + query_form + "->" + key_form,
        rounded,
        grad_context,
        preferred_element_type=jnp.float32,
    ).astype(jnp.bfloat16)
    grad_probs = jnp.einsum(
        query_form + "," + key_form + "->bhlm",
        grad_context,
        values,
        preferred_element_type=jnp.float32,
    )
    row_sums = jnp.sum(grad_probs * probabilities, axis=-1, keepdims=True)
    grad_scores = (probabilities * (grad_probs - row_sums) * scaling).astype(jnp.bfloat16)
    grad_queries = jnp.einsum(
        "bhlm," + key_form + "->" + query_form,
        grad_scores,
        key_rows,
        preferred_element_type=jnp.float32,
    ).astype(jnp.bfloat16)
    grad_keys = jnp.einsum(
        "bhlm," + query_form + "->" + key_form,
        grad_scores,
        queries,
        preferred_element_type=jnp.float32,
    ).astype(jnp.bfloat16)
    return (grad_queries, grad_keys, grad_values)


def times_transposed(left, weight):
    return lax.dot_general(
        left, weight, (((1,), (1,)), ((), ())), preferred_element_type=jnp.float32
    )


def regroup(arranged):
    return lax.all_to_all(arranged, "seq", split_axis=0, concat_axis=1, tiled=True)


def to_positions(matrix, stack_count):
    seq_count = lax.axis_size("seq")
    local_rows = matrix.shape[0] // seq_count
    col_count = matrix.shape[1] // stack_count
    arranged = matrix.reshape(seq_count, 1, local_rows, stack_count, col_count)
    return regroup(arranged)[0]


def to_frames(arranged):
    seq_count = lax.axis_size("seq")
    frame_count, local_rows, stack_count, col_count = arranged.shape
    returned = regroup(arranged.reshape(frame_count, 1, local_rows, stack_count, col_count))
    return returned.reshape(seq_count * local_rows, stack_count * col_count)


def per_device(
    clip,
    offsets,
    cotangent,
    gain_time,
    gain_space,
    proj_time,
    out_time,
    proj_space,
    out_space,
    bias_time,
    bias_space,
):
    proj_time, out_time, proj_space, out_space = (
        lax.all_gather(proj_time, "dp", axis=0, tiled=True),
        lax.all_gather(out_time, "dp", axis=0, tiled=True),
        lax.all_gather(proj_space, "dp", axis=0, tiled=True),
        lax.all_gather(out_space, "dp", axis=0, tiled=True),
    )
    bias_space = lax.all_gather(bias_space, "dp", axis=1, tiled=True)
    seq_count = lax.axis_size("seq")
    pos_count = clip.shape[1]
    local_rows = pos_count // seq_count
    head_cols = HEADS * HD
    hidden_in = clip[0].astype(jnp.float32) + offsets[0, 0].astype(jnp.float32)
    normed, inv_rms = rms_norm(hidden_in, gain_time)
    arranged_in = to_positions(normed, 1)
    flat_in = arranged_in.reshape(seq_count * local_rows, arranged_in.shape[-1])
    arranged = jnp.dot(flat_in, proj_time, preferred_element_type=jnp.float32).astype(jnp.bfloat16)
    arranged = arranged.reshape(seq_count, local_rows, 3, HEADS, HD)
    queries, key_rows, values = (arranged[:, :, 0], arranged[:, :, 1], arranged[:, :, 2])
    context, weights_time = attend(queries, key_rows, values, bias_time, True)
    context_frames = to_frames(context.reshape(seq_count, local_rows, 1, head_cols))
    after_time = hidden_in + jnp.dot(context_frames, out_time, preferred_element_type=jnp.float32)
    normed_space, inv_rms_space = rms_norm(after_time, gain_space)
    stacked_space = jnp.dot(normed_space, proj_space, preferred_element_type=jnp.float32).astype(
        jnp.bfloat16
    )
    stacked_space = stacked_space.reshape(1, pos_count, 3, HEADS, HD)
    queries_space, keys_space, values_space = (
        stacked_space[:, :, 0],
        stacked_space[:, :, 1],
        stacked_space[:, :, 2],
    )
    unused_context, weights_space = attend(
        queries_space, keys_space, values_space, bias_space, False
    )
    grad_out = cotangent[0, 0]
    grad_context = (
        times_transposed(grad_out, out_space).astype(jnp.bfloat16).reshape(1, pos_count, HEADS, HD)
    )
    grads_space = attend_back(
        queries_space, keys_space, values_space, weights_space, grad_context, False
    )
    grad_normed = times_transposed(
        jnp.stack(grads_space, axis=2).reshape(pos_count, 3 * head_cols), proj_space
    ).astype(jnp.bfloat16)
    grad_after = grad_out.astype(jnp.float32) + norm_back(
        after_time, inv_rms_space, gain_space, grad_normed
    )
    grad_context_time = times_transposed(grad_after.astype(jnp.bfloat16), out_time).astype(
        jnp.bfloat16
    )
    grad_context_pos = to_positions(grad_context_time, 1).reshape(seq_count, local_rows, HEADS, HD)
    grads_time = attend_back(queries, key_rows, values, weights_time, grad_context_pos, True)
    stacked_grads = jnp.stack(grads_time, axis=2)
    grad_pos = times_transposed(
        stacked_grads.reshape(seq_count * local_rows, 3 * head_cols), proj_time
    ).astype(jnp.bfloat16)
    grad_normed_time = to_frames(grad_pos.reshape(seq_count, local_rows, 1, grad_pos.shape[-1]))
    grad_in = grad_after + norm_back(hidden_in, inv_rms, gain_time, grad_normed_time)
    summed = lax.psum_scatter(
        grad_in.astype(jnp.bfloat16), "dp", scatter_dimension=0, tiled=True
    ).astype(jnp.float32)
    return summed[None]


LANES = 128
MASKED = -1e30


def dot_nn(left, right):
    return lax.dot_general(left, right, (((1,), (0,)), ((), ())), preferred_element_type=jnp.float32)


def dot_nt(left, right):
    return lax.dot_general(left, right, (((1,), (1,)), ((), ())), preferred_element_type=jnp.float32)


def dot_tn(left, right):
    return lax.dot_general(left, right, (((0,), (0,)), ((), ())), preferred_element_type=jnp.float32)


def pair_window(pair):
    first = 2 * pair * HD // LANES * LANES
    last = -(-2 * (pair + 1) * HD // LANES) * LANES
    return first, last


def head_lanes(head, first, last):
    lane = lax.broadcasted_iota(jnp.int32, (1, last - first), 1) + first
    return (lane >= head * HD) & (lane < (head + 1) * HD)


def two_heads(block, pair):
    first, last = pair_window(pair)
    piece = block[:, first:last]
    rows = [
        jnp.where(head_lanes(head, first, last), piece, jnp.zeros_like(piece))
        for head in (2 * pair, 2 * pair + 1)
    ]
    return jnp.concatenate(rows, axis=0)


def add_tiles(tiles, first, block):
    for col in range(0, block.shape[1], LANES):
        tile = (first + col) // LANES
        piece = block[:, col : col + LANES]
        tiles[tile] = piece if tiles[tile] is None else tiles[tile] + piece


def pick_tiles(blocks, tokens, tile_count):
    tiles = []
    for tile in range(tile_count):
        low, high = tile * LANES, (tile + 1) * LANES
        value = jnp.zeros((tokens, LANES), jnp.float32)
        for head in range(HEADS):
            if head * HD < high and (head + 1) * HD > low:
                first, _ = pair_window(head // 2)
                row = head % 2 * tokens
                piece = blocks[head // 2][row : row + tokens, low - first : high - first]
                value = jnp.where(head_lanes(head, low, high), piece, value)
        tiles.append(value)
    return tiles


def softmax_keys(scores, tokens):
    halves = []
    for row in range(0, scores.shape[0], tokens):
        block = scores[row : row + tokens]
        exp_block = jnp.exp(block - jnp.max(block, axis=0, keepdims=True))
        halves.append(exp_block * (1.0 / jnp.sum(exp_block, axis=0, keepdims=True)))
    return jnp.concatenate(halves, axis=0)


def score_grads(grad_probs, probs, tokens, scaling):
    halves = []
    for row in range(0, probs.shape[0], tokens):
        weights, grads = probs[row : row + tokens], grad_probs[row : row + tokens]
        mean = jnp.sum(grads * weights, axis=0, keepdims=True)
        halves.append((weights * (grads - mean) * scaling).astype(jnp.bfloat16))
    return jnp.concatenate(halves, axis=0)


def fused_kernel(
    seq_count,
    clip_in,
    off_in,
    cot_in,
    gain_time_in,
    gain_space_in,
    bias_time_in,
    proj_time_in,
    out_time_in,
    proj_space_in,
    out_space_in,
    bias_space_in,
    out_ref,
    clip_ref,
    off_ref,
    cot_ref,
    gain_time_ref,
    gain_space_ref,
    bias_time_ref,
    proj_time_t,
    out_time_t,
    proj_space_t,
    proj_time,
    out_time,
    proj_space,
    out_space,
    bias_space,
    bias_turned,
    bias_wide,
    hidden,
    after,
    q_time,
    k_time,
    v_time,
    probs_time,
    stacked,
    dc_space,
    dc_time,
    send_normed,
    got_normed,
    send_ctx,
    got_ctx,
    send_dc,
    got_dc,
    totals,
    pair_send,
    pair_got,
    send_back,
    got_back,
    after_send,
    after_got,
    send_sems,
    recv_sems,
    back_sems,
    weight_sems,
    weight_send_sems,
    weight_recv_sems,
    pair_send_sems,
    pair_recv_sems,
    input_sems,
):
    me = lax.axis_index("seq")
    core = lax.axis_index("dp")
    other = 1 - core
    tokens, width = hidden.shape
    rows = tokens // seq_count
    half = tokens // 2
    half_blocks = seq_count // 2
    wide = q_time.shape[1]
    scaling = 1.0 / math.sqrt(HD)

    barrier = pltpu.get_barrier_semaphore()
    for step in range(seq_count):
        peer = lax.rem(me + step, seq_count)
        if step:
            pl.semaphore_signal(
                barrier, inc=1, device_id=(peer, core), device_id_type=pl.DeviceIdType.MESH
            )
        pl.semaphore_signal(
            barrier, inc=1, device_id=(peer, other), device_id_type=pl.DeviceIdType.MESH
        )

    inputs = (clip_in, off_in, gain_time_in, cot_in, bias_time_in, gain_space_in)
    places = (clip_ref, off_ref, gain_time_ref, cot_ref, bias_time_ref, gain_space_ref)
    input_copies = [
        pltpu.make_async_copy(source, target, input_sems.at[place])
        for place, (source, target) in enumerate(zip(inputs, places))
    ]
    for copy in input_copies:
        copy.start()

    sources = (out_space_in, proj_time_in, out_time_in, proj_space_in)
    targets = (out_space, proj_time, out_time, proj_space)

    def part(place):
        if place == len(sources):
            count = bias_space_in.shape[1]
            start = pl.multiple_of(core * count, count)
            return bias_space_in, bias_space.at[:, pl.ds(start, count)]
        count = sources[place].shape[0]
        start = pl.multiple_of(core * count, count)
        return sources[place], targets[place].at[pl.ds(start, count)]

    weight_count = len(sources) + 1
    own_copies, pair_copies = [], []
    for place in range(weight_count):
        source, target = part(place)
        own_copies.append(pltpu.make_async_copy(source, target, weight_sems.at[place]))
        pair_copies.append(
            pltpu.make_async_remote_copy(
                src_ref=source,
                dst_ref=target,
                send_sem=weight_send_sems.at[place],
                recv_sem=weight_recv_sems.at[place],
                device_id=(me, other),
                device_id_type=pl.DeviceIdType.MESH,
            )
        )

    def weight_ready(place):
        own_copies[place].wait()
        pair_copies[place].wait_recv()

    def partner(step):
        place, bit = me, 1
        while bit <= step:
            if step & bit:
                place = place + bit * (1 - 2 * (me // bit % 2))
            bit *= 2
        return place

    def exchange(phase, sent, got, first, last):
        columns = pl.ds(first, last - first)

        def start():
            for step in range(seq_count - 1, -1, -1):
                target = partner(step)
                pltpu.make_async_remote_copy(
                    src_ref=sent.at[target, :, columns],
                    dst_ref=got.at[me, :, columns],
                    send_sem=send_sems.at[phase],
                    recv_sem=recv_sems.at[phase],
                    device_id=(target, other),
                    device_id_type=pl.DeviceIdType.MESH,
                ).start()

        def whole():
            return pltpu.make_async_remote_copy(
                src_ref=sent.at[:, :, columns],
                dst_ref=got.at[:, :, columns],
                send_sem=send_sems.at[phase],
                recv_sem=recv_sems.at[phase],
                device_id=(me, other),
                device_id_type=pl.DeviceIdType.MESH,
            )

        def arrive():
            whole().wait_recv()

        def finish():
            whole().wait_send()

        return start, arrive, finish

    def merged(ref, first=0, last=None):
        last = ref.shape[-1] if last is None else last
        block = ref[:, :, first:last].astype(jnp.float32)
        return block.reshape(tokens, last - first)

    def split(value):
        return value.reshape(seq_count, rows, value.shape[-1]).astype(jnp.bfloat16)

    def gain_row(gain_ref):
        pieces = [gain_ref[place : place + 1, :] for place in range(gain_ref.shape[0])]
        return jnp.concatenate(pieces, axis=1)

    def norm(value, gain_ref):
        inv_rms = lax.rsqrt(jnp.mean(value * value, axis=-1, keepdims=True) + epsilon)
        return value * inv_rms * gain_row(gain_ref), inv_rms

    def project(chunks, weight):
        head_cols = HEADS * HD
        whole = head_cols // LANES * LANES
        cuts = ((0, whole), (whole, 2 * head_cols), (2 * head_cols, 3 * head_cols))
        sums = None
        for first, last, give in chunks:
            block = give()
            terms = [dot_nn(block, weight[first:last, low:high]) for low, high in cuts]
            sums = terms if sums is None else [a + b for a, b in zip(sums, terms)]
        left, middle, values = sums
        queries = jnp.concatenate([left, middle[:, :LANES]], axis=1)
        key_rows = pltpu.roll(middle, middle.shape[1] - (head_cols - whole), 1)
        return queries.astype(jnp.bfloat16), key_rows.astype(jnp.bfloat16), values.astype(jnp.bfloat16)

    def stack_grads(dq, dk, dv):
        head_cols = HEADS * HD
        whole = head_cols // LANES * LANES
        count = len(dq)
        dq = jnp.concatenate(dq, axis=1)
        dk = pltpu.roll(jnp.concatenate(dk, axis=1), head_cols - whole, 1)
        dv = jnp.concatenate(dv, axis=1)
        stacked[:, :whole] = dq[:, :whole].astype(jnp.bfloat16)
        stacked[:, whole : whole + LANES] = (dq[:, whole:] + dk[:, :LANES]).astype(jnp.bfloat16)
        stacked[:, whole + LANES : 2 * head_cols] = dk[:, LANES:].astype(jnp.bfloat16)
        stacked[:, 2 * head_cols :] = dv[:, :head_cols].astype(jnp.bfloat16)

    def back(queries, key_rows, grad_ctx, values, probs, pairs):
        windows = [pair_window(pair) for pair in pairs]
        ctxs = [grad_ctx[:, first:last] for first, last in windows]
        grads = [dot_nt(two_heads(values, pair), ctx) for pair, ctx in zip(pairs, ctxs)]
        dv = [dot_nn(block.astype(jnp.bfloat16), ctx) for block, ctx in zip(probs, ctxs)]
        ds = [score_grads(grad, block, tokens, scaling) for grad, block in zip(grads, probs)]
        dk = [dot_nn(block, queries[:, first:last]) for block, (first, last) in zip(ds, windows)]
        dq = [dot_tn(block, two_heads(key_rows, pair)) for block, pair in zip(ds, pairs)]
        return dq, dk, dv

    def grads_of(parts):
        dq, dk, dv = (sum((part[place] for part in parts), []) for place in range(3))
        tiles = [None] * tile_count
        for pair, block in enumerate(dq):
            add_tiles(tiles, pair_window(pair)[0], block)
        return tiles, pick_tiles(dk, tokens, tile_count), pick_tiles(dv, tokens, tile_count)

    def turn(weight, turned):
        for first in range(0, weight.shape[0], LANES):
            turned[:, first : first + LANES] = weight[first : first + LANES, :].T

    tile_count = wide // LANES

    for copy in input_copies[:3]:
        copy.wait()
    for copy in own_copies:
        copy.start()
    hidden[...] = clip_ref[...].astype(jnp.float32) + off_ref[...].astype(jnp.float32)
    normed, inv_time = norm(hidden[...], gain_time_ref)
    send_normed[...] = split(normed)
    pl.semaphore_wait(barrier, 2 * seq_count - 1)
    feature_cuts = [0, width // (2 * LANES) * LANES + LANES, width]
    chunk_count = len(feature_cuts) - 1
    normed_moves = [
        exchange(place, send_normed, got_normed, feature_cuts[place], feature_cuts[place + 1])
        for place in range(chunk_count)
    ]
    for start, _, _ in normed_moves:
        start()
    for copy in pair_copies:
        copy.start()

    extra = wide - HEADS * HD
    for ref in (out_time, out_space):
        ref[pl.ds(HEADS * HD, extra), :] = jnp.zeros((extra, width), jnp.bfloat16)
    frame = lax.broadcasted_iota(jnp.int32, (seq_count, tokens), 0)
    column = lax.broadcasted_iota(jnp.int32, (seq_count, tokens), 1)
    spread = jnp.where(column // rows == frame, 1.0, 0.0).astype(jnp.float32)
    same = lax.broadcasted_iota(jnp.int32, (tokens, tokens), 0) % rows == (
        lax.broadcasted_iota(jnp.int32, (tokens, tokens), 1) % rows
    )
    for copy in input_copies[3:]:
        copy.wait()
    for head in range(HEADS):
        block = lax.dot_general(
            bias_time_ref[head * seq_count : (head + 1) * seq_count, :],
            spread,
            (((0,), (0,)), ((), ())),
            precision=lax.Precision.HIGHEST,
            preferred_element_type=jnp.float32,
        )
        block = jnp.broadcast_to(block[:, None, :], (seq_count, rows, tokens))
        row = head % 2 * tokens
        bias_wide[head // 2, row : row + tokens, :] = jnp.where(
            same, block.reshape(tokens, tokens), MASKED
        )

    weight_ready(0)
    dc_space[...] = dot_nt(cot_ref[...], out_space[...]).astype(jnp.bfloat16)

    weight_ready(1)

    def arrived(place):
        normed_moves[place][1]()
        return merged(got_normed, feature_cuts[place], feature_cuts[place + 1]).astype(jnp.bfloat16)

    queries, key_rows, values = project(
        [
            (feature_cuts[place], feature_cuts[place + 1], functools.partial(arrived, place))
            for place in range(chunk_count)
        ],
        proj_time,
    )
    q_time[...] = queries
    k_time[...] = key_rows
    v_time[:, : HEADS * HD] = values
    ctx = [None] * tile_count
    cut = 2 * LANES
    ctx_moves = [
        exchange(chunk_count, send_ctx, got_ctx, 0, cut),
        exchange(chunk_count + 1, send_ctx, got_ctx, cut, wide),
    ]
    pair_count = HEADS // 2

    def probabilities(queries, key_rows, bias, pairs):
        scores = []
        for pair in pairs:
            first, last = pair_window(pair)
            scores.append(dot_nt(two_heads(key_rows, pair), queries[:, first:last]))
        return [
            softmax_keys(block * scaling + bias[pair], tokens) for pair, block in zip(pairs, scores)
        ]

    groups = [range(place, place + 2) for place in range(0, pair_count, 2)]
    for group in groups:
        probs = probabilities(q_time, k_time, bias_wide, group)
        for pair, block in zip(group, probs):
            probs_time[pair] = block
            add_tiles(
                ctx,
                pair_window(pair)[0],
                dot_tn(block.astype(jnp.bfloat16), two_heads(v_time, pair)),
            )
        if group is groups[0]:
            send_ctx[:, :, :cut] = split(jnp.concatenate(ctx[: cut // LANES], axis=1))
            ctx_moves[0][0]()
    send_ctx[:, :, cut:] = split(jnp.concatenate(ctx[cut // LANES :], axis=1))
    ctx_moves[1][0]()
    weight_ready(2)
    weight_ready(3)
    weight_ready(4)
    turn(proj_space, proj_space_t)
    turn(out_time, out_time_t)
    for head in range(HEADS):
        row = head % 2 * tokens
        bias_turned[head // 2, row : row + tokens, :] = bias_space[head].T
    ctx_moves[0][1]()
    first_part = dot_nn(merged(got_ctx, 0, cut).astype(jnp.bfloat16), out_time[:cut])
    ctx_moves[1][1]()

    second_part = dot_nn(merged(got_ctx, cut, wide).astype(jnp.bfloat16), out_time[cut:])
    after[...] = hidden[...] + (first_part + second_part)
    normed, inv_space = norm(after[...], gain_space_ref)
    queries, key_rows, values = project(
        [(0, width, lambda: normed.astype(jnp.bfloat16))], proj_space
    )
    values = jnp.concatenate([values, jnp.zeros((tokens, extra), jnp.bfloat16)], axis=1)
    parts = []
    for group in groups:
        probs = probabilities(queries, key_rows, bias_turned, group)
        parts.append(back(queries, key_rows, dc_space, values, probs, group))
    stack_grads(*grads_of(parts))
    grad_normed = dot_nn(stacked[...], proj_space_t[...]).astype(jnp.bfloat16)
    weighted = grad_normed.astype(jnp.float32) * gain_row(gain_space_ref)
    cubed = inv_space * inv_space * inv_space
    mean_wh = jnp.mean(weighted * after[...], axis=-1, keepdims=True)
    grad_after = cot_ref[...].astype(jnp.float32) + (
        inv_space * weighted - after[...] * cubed * mean_wh
    )
    after[...] = grad_after

    rounded = grad_after.astype(jnp.bfloat16)
    dc_moves = [
        exchange(chunk_count + 2, send_dc, got_dc, 0, cut),
        exchange(chunk_count + 3, send_dc, got_dc, cut, wide),
    ]
    send_dc[:, :, :cut] = split(dot_nn(rounded, out_time_t[:, :cut]))
    dc_moves[0][0]()
    grad_ctx = dot_nn(rounded, out_time_t[:, cut:])
    lane = lax.broadcasted_iota(jnp.int32, (1, wide - cut), 1) + cut
    high = inv_time.astype(jnp.bfloat16).astype(jnp.float32)
    spare = jnp.where(lane < HEADS * HD + extra // 2, high, inv_time - high)
    send_dc[:, :, cut:] = split(jnp.where(lane < HEADS * HD, grad_ctx, spare))
    dc_moves[1][0]()
    after_send[...] = after[pl.ds(pl.multiple_of(other * half, half), half), :].astype(jnp.bfloat16)

    def pair_copy(place, source, target):
        return pltpu.make_async_remote_copy(
            src_ref=source,
            dst_ref=target,
            send_sem=pair_send_sems.at[place],
            recv_sem=pair_recv_sems.at[place],
            device_id=(me, other),
            device_id_type=pl.DeviceIdType.MESH,
        )

    after_copy = pair_copy(0, after_send, after_got)
    after_copy.start()

    turn(proj_time, proj_time_t)
    dc_moves[0][1]()
    dc_time[:, :cut] = merged(got_dc, 0, cut).astype(jnp.bfloat16)
    dc_moves[1][1]()
    rest = merged(got_dc, cut, wide)
    place = HEADS * HD - cut
    inv_rows = rest[:, place : place + 1] + rest[:, wide - cut - 1 :]
    dc_time[:, cut:] = rest.astype(jnp.bfloat16)
    parts = []
    for group in groups:
        probs = [probs_time[pair] for pair in group]
        parts.append(back(q_time, k_time, dc_time, v_time, probs, group))
    stack_grads(*grads_of(parts))
    grad_normed = dot_nn(stacked[...], proj_time_t[...]).astype(jnp.bfloat16).astype(jnp.float32)
    normed = merged(got_normed)
    gain = gain_row(gain_time_ref)
    mean_dn = jnp.mean(grad_normed * normed, axis=-1, keepdims=True)
    total = inv_rows * (
        grad_normed * gain - normed * (1.0 / gain) * mean_dn
    )
    totals[...] = total.reshape(seq_count, rows, width)

    pair_send[...] = totals[pl.ds(core * half_blocks, half_blocks)].astype(jnp.bfloat16)
    total_copy = pair_copy(1, pair_send, pair_got)
    total_copy.start()
    total_copy.wait_recv()
    send_back[...] = (
        totals[pl.ds(other * half_blocks, half_blocks)] + pair_got[...].astype(jnp.float32)
    ).astype(jnp.bfloat16)
    my_slot = lax.rem(me, half_blocks)
    my_half = me // half_blocks

    for slot in range(half_blocks):
        pltpu.make_async_remote_copy(
            src_ref=send_back.at[slot],
            dst_ref=got_back.at[my_slot],
            send_sem=back_sems.at[0],
            recv_sem=back_sems.at[1],
            device_id=(other * half_blocks + slot, my_half),
            device_id_type=pl.DeviceIdType.MESH,
        ).start()
    whole_back = pltpu.make_async_remote_copy(
        src_ref=send_back,
        dst_ref=got_back,
        send_sem=back_sems.at[0],
        recv_sem=back_sems.at[1],
        device_id=(me, other),
        device_id_type=pl.DeviceIdType.MESH,
    )
    after_copy.wait_recv()
    whole_back.wait_recv()
    out_ref[...] = (
        after[pl.ds(pl.multiple_of(core * half, half), half), :]
        + after_got[...].astype(jnp.float32)
        + got_back[...].astype(jnp.float32).reshape(half, width)
    )
    whole_back.wait_send()
    for _, _, finish in (*normed_moves, *ctx_moves, *dc_moves):
        finish()
    for copy in (*pair_copies, after_copy, total_copy):
        copy.wait_send()


def fused_device(
    clip,
    offsets,
    cotangent,
    gain_time,
    gain_space,
    proj_time,
    out_time,
    proj_space,
    out_space,
    bias_time,
    bias_space,
):
    seq_count = lax.axis_size("seq")
    tokens, width = clip.shape[1:]
    rows = tokens // seq_count
    head_cols = HEADS * HD
    wide = -(-head_cols // LANES) * LANES
    half, half_blocks = tokens // 2, seq_count // 2
    moves = 6
    f32, bf16 = jnp.float32, jnp.bfloat16
    vmem = pltpu.VMEM
    dma = pltpu.SemaphoreType.DMA
    scratch = [
        vmem((tokens, width), bf16),
        vmem((tokens, width), bf16),
        vmem((tokens, width), bf16),
        vmem((width // LANES, LANES), f32),
        vmem((width // LANES, LANES), f32),
        vmem((HEADS * seq_count, seq_count), f32),
        vmem((3 * head_cols, width), bf16),
        vmem((width, wide), bf16),
        vmem((3 * head_cols, width), bf16),
        vmem((width, 3 * head_cols), bf16),
        vmem((wide, width), bf16),
        vmem((width, 3 * head_cols), bf16),
        vmem((wide, width), bf16),
        vmem((HEADS, tokens, tokens), f32),
        vmem((HEADS // 2, 2 * tokens, tokens), f32),
        vmem((HEADS // 2, 2 * tokens, tokens), f32),
        vmem((tokens, width), f32),
        vmem((tokens, width), f32),
        vmem((tokens, wide), bf16),
        vmem((tokens, wide), bf16),
        vmem((tokens, wide), bf16),
        vmem((HEADS // 2, 2 * tokens, tokens), f32),
        vmem((tokens, 3 * head_cols), bf16),
        vmem((tokens, wide), bf16),
        vmem((tokens, wide), bf16),
        vmem((seq_count, rows, width), bf16),
        vmem((seq_count, rows, width), bf16),
        vmem((seq_count, rows, wide), bf16),
        vmem((seq_count, rows, wide), bf16),
        vmem((seq_count, rows, wide), bf16),
        vmem((seq_count, rows, wide), bf16),
        vmem((seq_count, rows, width), f32),
        vmem((half_blocks, rows, width), bf16),
        vmem((half_blocks, rows, width), bf16),
        vmem((half_blocks, rows, width), bf16),
        vmem((half_blocks, rows, width), bf16),
        vmem((half, width), bf16),
        vmem((half, width), bf16),
        dma((moves,)),
        dma((moves,)),
        dma((2,)),
        dma((5,)),
        dma((5,)),
        dma((5,)),
        dma((2,)),
        dma((2,)),
        dma((6,)),
    ]
    out_vmem = pl.BlockSpec(memory_space=pltpu.VMEM)
    anywhere = pl.BlockSpec(memory_space=pl.ANY)
    out = pl.pallas_call(
        functools.partial(fused_kernel, seq_count),
        out_shape=pltpu.VMEM((half, width), f32),
        in_specs=[anywhere] * 11,
        out_specs=out_vmem,
        scratch_shapes=scratch,
        compiler_params=pltpu.CompilerParams(
            collective_id=0, has_side_effects=True, vmem_limit_bytes=56 * 1024 * 1024
        ),
    )(
        clip[0],
        offsets[0, 0],
        cotangent[0, 0],
        gain_time.reshape(-1, LANES),
        gain_space.reshape(-1, LANES),
        bias_time.reshape(HEADS * bias_time.shape[1], bias_time.shape[2]),
        proj_time,
        out_time,
        proj_space,
        out_space,
        bias_space,
    )
    return out[None]


def on_device(clip, *rest):
    seq_count = lax.axis_size("seq")
    tokens = clip.shape[1]
    fits = (
        lax.axis_size("dp") == 2
        and clip.shape[0] == 1
        and seq_count & (seq_count - 1) == 0
        and tokens == 8 * seq_count
        and tokens == LANES
        and clip.shape[2] % LANES == 0
    )
    return (fused_device if fits else per_device)(clip, *rest)


def solution(mesh):
    in_specs = (
        P("seq", None, None),
        P("dp", "seq", None, None),
        P("dp", "seq", None, None),
        P(),
        P(),
        P("dp", None),
        P("dp", None),
        P("dp", None),
        P("dp", None),
        P(),
        P(None, "dp", None),
    )
    out_specs = P("seq", "dp", None)
    return jax.shard_map(
        on_device, mesh=mesh, in_specs=in_specs, out_specs=out_specs, check_vma=False
    )
```

```python
import functools
import math

import jax
import jax.numpy as jnp
from jax import lax
from jax.experimental import pallas as pl
from jax.experimental.pallas import tpu as pltpu
from jax.sharding import PartitionSpec as P

HEADS = 8
HD = 72


epsilon = 1e-06


def rms_norm(hidden_in, gain_vec):
    inv_rms = lax.rsqrt(jnp.mean(hidden_in * hidden_in, axis=-1, keepdims=True) + epsilon)
    return ((hidden_in * inv_rms * gain_vec).astype(jnp.bfloat16), inv_rms)


def norm_back(hidden_in, inv_rms, gain_vec, grad_normed):
    weighted = grad_normed.astype(jnp.float32) * gain_vec
    cubed = inv_rms * inv_rms * inv_rms
    return inv_rms * weighted - hidden_in * cubed * jnp.mean(
        weighted * hidden_in, axis=-1, keepdims=True
    )


def layout_forms(frame_major):
    if frame_major:
        return ("lbhe", "mbhe")
    return ("blhe", "bmhe")


def attend(queries, key_rows, values, score_bias, frame_major):
    query_form, key_form = layout_forms(frame_major)
    scaling = 1.0 / math.sqrt(queries.shape[-1])
    scores = (
        jnp.einsum(
            query_form + "," + key_form + "->bhlm",
            queries,
            key_rows,
            preferred_element_type=jnp.float32,
        )
        * scaling
        + score_bias
    )
    highest = jnp.max(scores, axis=-1, keepdims=True)
    exp_scores = jnp.exp(scores - highest)
    probabilities = exp_scores / jnp.sum(exp_scores, axis=-1, keepdims=True)
    context = jnp.einsum(
        "bhlm," + key_form + "->" + query_form,
        probabilities.astype(jnp.bfloat16),
        values,
        preferred_element_type=jnp.float32,
    )
    return (context.astype(jnp.bfloat16), probabilities)


def attend_back(queries, key_rows, values, probabilities, grad_context, frame_major):
    query_form, key_form = layout_forms(frame_major)
    scaling = 1.0 / math.sqrt(queries.shape[-1])
    rounded = probabilities.astype(jnp.bfloat16)
    grad_values = jnp.einsum(
        "bhlm," + query_form + "->" + key_form,
        rounded,
        grad_context,
        preferred_element_type=jnp.float32,
    ).astype(jnp.bfloat16)
    grad_probs = jnp.einsum(
        query_form + "," + key_form + "->bhlm",
        grad_context,
        values,
        preferred_element_type=jnp.float32,
    )
    row_sums = jnp.sum(grad_probs * probabilities, axis=-1, keepdims=True)
    grad_scores = (probabilities * (grad_probs - row_sums) * scaling).astype(jnp.bfloat16)
    grad_queries = jnp.einsum(
        "bhlm," + key_form + "->" + query_form,
        grad_scores,
        key_rows,
        preferred_element_type=jnp.float32,
    ).astype(jnp.bfloat16)
    grad_keys = jnp.einsum(
        "bhlm," + query_form + "->" + key_form,
        grad_scores,
        queries,
        preferred_element_type=jnp.float32,
    ).astype(jnp.bfloat16)
    return (grad_queries, grad_keys, grad_values)


def times_transposed(left, weight):
    return lax.dot_general(
        left, weight, (((1,), (1,)), ((), ())), preferred_element_type=jnp.float32
    )


def regroup(arranged):
    return lax.all_to_all(arranged, "seq", split_axis=0, concat_axis=1, tiled=True)


def to_positions(matrix, stack_count):
    seq_count = lax.axis_size("seq")
    local_rows = matrix.shape[0] // seq_count
    col_count = matrix.shape[1] // stack_count
    arranged = matrix.reshape(seq_count, 1, local_rows, stack_count, col_count)
    return regroup(arranged)[0]


def to_frames(arranged):
    seq_count = lax.axis_size("seq")
    frame_count, local_rows, stack_count, col_count = arranged.shape
    returned = regroup(arranged.reshape(frame_count, 1, local_rows, stack_count, col_count))
    return returned.reshape(seq_count * local_rows, stack_count * col_count)


def per_device(
    clip,
    offsets,
    cotangent,
    gain_time,
    gain_space,
    proj_time,
    out_time,
    proj_space,
    out_space,
    bias_time,
    bias_space,
):
    proj_time, out_time, proj_space, out_space = (
        lax.all_gather(proj_time, "dp", axis=0, tiled=True),
        lax.all_gather(out_time, "dp", axis=0, tiled=True),
        lax.all_gather(proj_space, "dp", axis=0, tiled=True),
        lax.all_gather(out_space, "dp", axis=0, tiled=True),
    )
    bias_space = lax.all_gather(bias_space, "dp", axis=1, tiled=True)
    seq_count = lax.axis_size("seq")
    pos_count = clip.shape[1]
    local_rows = pos_count // seq_count
    head_cols = HEADS * HD
    hidden_in = clip[0].astype(jnp.float32) + offsets[0, 0].astype(jnp.float32)
    normed, inv_rms = rms_norm(hidden_in, gain_time)
    arranged_in = to_positions(normed, 1)
    flat_in = arranged_in.reshape(seq_count * local_rows, arranged_in.shape[-1])
    arranged = jnp.dot(flat_in, proj_time, preferred_element_type=jnp.float32).astype(jnp.bfloat16)
    arranged = arranged.reshape(seq_count, local_rows, 3, HEADS, HD)
    queries, key_rows, values = (arranged[:, :, 0], arranged[:, :, 1], arranged[:, :, 2])
    context, weights_time = attend(queries, key_rows, values, bias_time, True)
    context_frames = to_frames(context.reshape(seq_count, local_rows, 1, head_cols))
    after_time = hidden_in + jnp.dot(context_frames, out_time, preferred_element_type=jnp.float32)
    normed_space, inv_rms_space = rms_norm(after_time, gain_space)
    stacked_space = jnp.dot(normed_space, proj_space, preferred_element_type=jnp.float32).astype(
        jnp.bfloat16
    )
    stacked_space = stacked_space.reshape(1, pos_count, 3, HEADS, HD)
    queries_space, keys_space, values_space = (
        stacked_space[:, :, 0],
        stacked_space[:, :, 1],
        stacked_space[:, :, 2],
    )
    unused_context, weights_space = attend(
        queries_space, keys_space, values_space, bias_space, False
    )
    grad_out = cotangent[0, 0]
    grad_context = (
        times_transposed(grad_out, out_space).astype(jnp.bfloat16).reshape(1, pos_count, HEADS, HD)
    )
    grads_space = attend_back(
        queries_space, keys_space, values_space, weights_space, grad_context, False
    )
    grad_normed = times_transposed(
        jnp.stack(grads_space, axis=2).reshape(pos_count, 3 * head_cols), proj_space
    ).astype(jnp.bfloat16)
    grad_after = grad_out.astype(jnp.float32) + norm_back(
        after_time, inv_rms_space, gain_space, grad_normed
    )
    grad_context_time = times_transposed(grad_after.astype(jnp.bfloat16), out_time).astype(
        jnp.bfloat16
    )
    grad_context_pos = to_positions(grad_context_time, 1).reshape(seq_count, local_rows, HEADS, HD)
    grads_time = attend_back(queries, key_rows, values, weights_time, grad_context_pos, True)
    stacked_grads = jnp.stack(grads_time, axis=2)
    grad_pos = times_transposed(
        stacked_grads.reshape(seq_count * local_rows, 3 * head_cols), proj_time
    ).astype(jnp.bfloat16)
    grad_normed_time = to_frames(grad_pos.reshape(seq_count, local_rows, 1, grad_pos.shape[-1]))
    grad_in = grad_after + norm_back(hidden_in, inv_rms, gain_time, grad_normed_time)
    summed = lax.psum_scatter(
        grad_in.astype(jnp.bfloat16), "dp", scatter_dimension=0, tiled=True
    ).astype(jnp.float32)
    return summed[None]


LANES = 128
MASKED = -1e30


def dot_nn(left, right):
    return lax.dot_general(left, right, (((1,), (0,)), ((), ())), preferred_element_type=jnp.float32)


def dot_nt(left, right):
    return lax.dot_general(left, right, (((1,), (1,)), ((), ())), preferred_element_type=jnp.float32)


def dot_tn(left, right):
    return lax.dot_general(left, right, (((0,), (0,)), ((), ())), preferred_element_type=jnp.float32)


def pair_window(pair):
    first = 2 * pair * HD // LANES * LANES
    last = -(-2 * (pair + 1) * HD // LANES) * LANES
    return first, last


def head_lanes(head, first, last):
    lane = lax.broadcasted_iota(jnp.int32, (1, last - first), 1) + first
    return (lane >= head * HD) & (lane < (head + 1) * HD)


def two_heads(block, pair):
    first, last = pair_window(pair)
    piece = block[:, first:last]
    rows = [
        jnp.where(head_lanes(head, first, last), piece, jnp.zeros_like(piece))
        for head in (2 * pair, 2 * pair + 1)
    ]
    return jnp.concatenate(rows, axis=0)


def add_tiles(tiles, first, block):
    for col in range(0, block.shape[1], LANES):
        tile = (first + col) // LANES
        piece = block[:, col : col + LANES]
        tiles[tile] = piece if tiles[tile] is None else tiles[tile] + piece


def pick_tiles(blocks, tokens, tile_count):
    tiles = []
    for tile in range(tile_count):
        low, high = tile * LANES, (tile + 1) * LANES
        value = jnp.zeros((tokens, LANES), jnp.float32)
        for head in range(HEADS):
            if head * HD < high and (head + 1) * HD > low:
                first, _ = pair_window(head // 2)
                row = head % 2 * tokens
                piece = blocks[head // 2][row : row + tokens, low - first : high - first]
                value = jnp.where(head_lanes(head, low, high), piece, value)
        tiles.append(value)
    return tiles


def softmax_keys(scores, tokens):
    halves = []
    for row in range(0, scores.shape[0], tokens):
        block = scores[row : row + tokens]
        exp_block = jnp.exp(block - jnp.max(block, axis=0, keepdims=True))
        halves.append(exp_block * (1.0 / jnp.sum(exp_block, axis=0, keepdims=True)))
    return jnp.concatenate(halves, axis=0)


def score_grads(grad_probs, probs, tokens, scaling):
    halves = []
    for row in range(0, probs.shape[0], tokens):
        weights, grads = probs[row : row + tokens], grad_probs[row : row + tokens]
        mean = jnp.sum(grads * weights, axis=0, keepdims=True)
        halves.append((weights * (grads - mean) * scaling).astype(jnp.bfloat16))
    return jnp.concatenate(halves, axis=0)


def fused_kernel(
    seq_count,
    clip_in,
    off_in,
    cot_in,
    gain_time_in,
    gain_space_in,
    bias_time_in,
    proj_time_in,
    out_time_in,
    proj_space_in,
    out_space_in,
    bias_space_in,
    out_ref,
    clip_ref,
    off_ref,
    cot_ref,
    gain_time_ref,
    gain_space_ref,
    bias_time_ref,
    proj_time_t,
    out_time_t,
    proj_space_t,
    proj_time,
    out_time,
    proj_space,
    out_space,
    bias_space,
    bias_turned,
    bias_wide,
    fold_in,
    fold,
    fold_t,
    base,
    hidden,
    after,
    q_time,
    k_time,
    v_time,
    probs_time,
    stacked,
    dc_space,
    dc_time,
    send_normed,
    got_normed,
    send_ctx,
    got_ctx,
    send_dc,
    got_dc,
    totals,
    pair_send,
    pair_got,
    send_back,
    got_back,
    after_send,
    after_got,
    send_sems,
    recv_sems,
    back_sems,
    weight_sems,
    weight_send_sems,
    weight_recv_sems,
    pair_send_sems,
    pair_recv_sems,
    input_sems,
):
    me = lax.axis_index("seq")
    core = lax.axis_index("dp")
    other = 1 - core
    tokens, width = hidden.shape
    rows = tokens // seq_count
    half = tokens // 2
    half_blocks = seq_count // 2
    wide = q_time.shape[1]
    scaling = 1.0 / math.sqrt(HD)

    barrier = pltpu.get_barrier_semaphore()
    for step in range(seq_count):
        peer = lax.rem(me + step, seq_count)
        if step:
            pl.semaphore_signal(
                barrier, inc=1, device_id=(peer, core), device_id_type=pl.DeviceIdType.MESH
            )
        pl.semaphore_signal(
            barrier, inc=1, device_id=(peer, other), device_id_type=pl.DeviceIdType.MESH
        )

    inputs = (clip_in, off_in, gain_time_in, cot_in, bias_time_in, gain_space_in)
    places = (clip_ref, off_ref, gain_time_ref, cot_ref, bias_time_ref, gain_space_ref)
    input_copies = [
        pltpu.make_async_copy(source, target, input_sems.at[place])
        for place, (source, target) in enumerate(zip(inputs, places))
    ]
    for copy in input_copies:
        copy.start()

    sources = (out_space_in, proj_time_in, out_time_in, proj_space_in)
    targets = (out_space, proj_time, out_time, proj_space)

    def part(place):
        if place == len(sources):
            count = bias_space_in.shape[1]
            start = pl.multiple_of(core * count, count)
            return bias_space_in, bias_space.at[:, pl.ds(start, count)]
        count = sources[place].shape[0]
        start = pl.multiple_of(core * count, count)
        return sources[place], targets[place].at[pl.ds(start, count)]

    weight_count = len(sources) + 1
    own_copies, pair_copies = [], []
    for place in range(weight_count):
        source, target = part(place)
        own_copies.append(pltpu.make_async_copy(source, target, weight_sems.at[place]))
        pair_copies.append(
            pltpu.make_async_remote_copy(
                src_ref=source,
                dst_ref=target,
                send_sem=weight_send_sems.at[place],
                recv_sem=weight_recv_sems.at[place],
                device_id=(me, other),
                device_id_type=pl.DeviceIdType.MESH,
            )
        )

    def weight_ready(place):
        own_copies[place].wait()
        pair_copies[place].wait_recv()

    def partner(step):
        place, bit = me, 1
        while bit <= step:
            if step & bit:
                place = place + bit * (1 - 2 * (me // bit % 2))
            bit *= 2
        return place

    def exchange(phase, sent, got, first, last):
        columns = pl.ds(first, last - first)

        def start():
            for step in range(seq_count - 1, -1, -1):
                target = partner(step)
                pltpu.make_async_remote_copy(
                    src_ref=sent.at[target, :, columns],
                    dst_ref=got.at[me, :, columns],
                    send_sem=send_sems.at[phase],
                    recv_sem=recv_sems.at[phase],
                    device_id=(target, other),
                    device_id_type=pl.DeviceIdType.MESH,
                ).start()

        def whole():
            return pltpu.make_async_remote_copy(
                src_ref=sent.at[:, :, columns],
                dst_ref=got.at[:, :, columns],
                send_sem=send_sems.at[phase],
                recv_sem=recv_sems.at[phase],
                device_id=(me, other),
                device_id_type=pl.DeviceIdType.MESH,
            )

        def arrive():
            whole().wait_recv()

        def finish():
            whole().wait_send()

        return start, arrive, finish

    def merged(ref, first=0, last=None):
        last = ref.shape[-1] if last is None else last
        block = ref[:, :, first:last].astype(jnp.float32)
        return block.reshape(tokens, last - first)

    def split(value):
        return value.reshape(seq_count, rows, value.shape[-1]).astype(jnp.bfloat16)

    def gain_row(gain_ref):
        pieces = [gain_ref[place : place + 1, :] for place in range(gain_ref.shape[0])]
        return jnp.concatenate(pieces, axis=1)

    def norm(value, gain_ref):
        inv_rms = lax.rsqrt(jnp.mean(value * value, axis=-1, keepdims=True) + epsilon)
        return value * inv_rms * gain_row(gain_ref), inv_rms

    head_cols = HEADS * HD
    whole_cols = head_cols // LANES * LANES
    cuts = ((0, whole_cols), (whole_cols, 2 * head_cols), (2 * head_cols, 3 * head_cols))

    def project(block, weight):
        return [dot_nn(block, weight[:, low:high]) for low, high in cuts]

    def add(sums, terms):
        return [a + b for a, b in zip(sums, terms)]

    def by_heads(sums):
        left, middle, values = sums
        queries = jnp.concatenate([left, middle[:, :LANES]], axis=1)
        key_rows = pltpu.roll(middle, middle.shape[1] - (head_cols - whole_cols), 1)
        return queries.astype(jnp.bfloat16), key_rows.astype(jnp.bfloat16), values.astype(jnp.bfloat16)

    def weighted_sum(grads, stacks):
        total = None
        for tiles, stack in zip(grads, stacks):
            for tile, value in enumerate(tiles):
                term = value * stack[:, tile * LANES : (tile + 1) * LANES].astype(jnp.float32)
                total = term if total is None else total + term
        return jnp.sum(total, axis=-1, keepdims=True)

    def stack_grads(dq, dk, dv):
        whole = whole_cols
        dq = jnp.concatenate(dq, axis=1)
        dk = pltpu.roll(jnp.concatenate(dk, axis=1), head_cols - whole, 1)
        dv = jnp.concatenate(dv, axis=1)
        stacked[:, :whole] = dq[:, :whole].astype(jnp.bfloat16)
        stacked[:, whole : whole + LANES] = (dq[:, whole:] + dk[:, :LANES]).astype(jnp.bfloat16)
        stacked[:, whole + LANES : 2 * head_cols] = dk[:, LANES:].astype(jnp.bfloat16)
        stacked[:, 2 * head_cols :] = dv[:, :head_cols].astype(jnp.bfloat16)

    def back(queries, key_rows, grad_ctx, values, probs, pairs):
        windows = [pair_window(pair) for pair in pairs]
        ctxs = [grad_ctx[:, first:last] for first, last in windows]
        grads = [dot_nt(two_heads(values, pair), ctx) for pair, ctx in zip(pairs, ctxs)]
        dv = [dot_nn(block.astype(jnp.bfloat16), ctx) for block, ctx in zip(probs, ctxs)]
        ds = [score_grads(grad, block, tokens, scaling) for grad, block in zip(grads, probs)]
        dk = [dot_nn(block, queries[:, first:last]) for block, (first, last) in zip(ds, windows)]
        dq = [dot_tn(block, two_heads(key_rows, pair)) for block, pair in zip(ds, pairs)]
        return dq, dk, dv

    def grads_of(parts):
        dq, dk, dv = (sum((part[place] for part in parts), []) for place in range(3))
        tiles = [None] * tile_count
        for pair, block in enumerate(dq):
            add_tiles(tiles, pair_window(pair)[0], block)
        return tiles, pick_tiles(dk, tokens, tile_count), pick_tiles(dv, tokens, tile_count)

    def turn(weight, turned):
        for first in range(0, weight.shape[0], LANES):
            turned[:, first : first + LANES] = weight[first : first + LANES, :].T

    tile_count = wide // LANES

    for copy in input_copies[:3]:
        copy.wait()
    for copy in own_copies:
        copy.start()
    hidden[...] = clip_ref[...].astype(jnp.float32) + off_ref[...].astype(jnp.float32)
    normed, inv_time = norm(hidden[...], gain_time_ref)
    send_normed[...] = split(normed)
    pl.semaphore_wait(barrier, 2 * seq_count - 1)
    feature_cuts = [0, width // (2 * LANES) * LANES + LANES, width]
    chunk_count = len(feature_cuts) - 1
    normed_moves = [
        exchange(place, send_normed, got_normed, feature_cuts[place], feature_cuts[place + 1])
        for place in range(chunk_count)
    ]
    for start, _, _ in normed_moves:
        start()
    for copy in pair_copies:
        copy.start()

    extra = wide - HEADS * HD
    for ref in (out_time, out_space):
        ref[pl.ds(HEADS * HD, extra), :] = jnp.zeros((extra, width), jnp.bfloat16)
    frame = lax.broadcasted_iota(jnp.int32, (seq_count, tokens), 0)
    column = lax.broadcasted_iota(jnp.int32, (seq_count, tokens), 1)
    spread = jnp.where(column // rows == frame, 1.0, 0.0).astype(jnp.float32)
    same = lax.broadcasted_iota(jnp.int32, (tokens, tokens), 0) % rows == (
        lax.broadcasted_iota(jnp.int32, (tokens, tokens), 1) % rows
    )
    for copy in input_copies[3:]:
        copy.wait()
    for head in range(HEADS):
        block = lax.dot_general(
            bias_time_ref[head * seq_count : (head + 1) * seq_count, :],
            spread,
            (((0,), (0,)), ((), ())),
            precision=lax.Precision.HIGHEST,
            preferred_element_type=jnp.float32,
        )
        block = jnp.broadcast_to(block[:, None, :], (seq_count, rows, tokens))
        row = head % 2 * tokens
        bias_wide[head // 2, row : row + tokens, :] = jnp.where(
            same, block.reshape(tokens, tokens), MASKED
        )

    weight_ready(0)
    dc_space[...] = dot_nt(cot_ref[...], out_space[...]).astype(jnp.bfloat16)

    weight_ready(1)

    def arrived(place):
        normed_moves[place][1]()
        return merged(got_normed, feature_cuts[place], feature_cuts[place + 1]).astype(jnp.bfloat16)

    sums = project(arrived(0), proj_time.at[: feature_cuts[1]])
    for place in range(1, chunk_count):
        rows_of = proj_time.at[feature_cuts[place] : feature_cuts[place + 1]]
        sums = add(sums, project(arrived(place), rows_of))
    queries, key_rows, values = by_heads(sums)
    q_time[...] = queries
    k_time[...] = key_rows
    v_time[:, : HEADS * HD] = values
    v_time[:, HEADS * HD :] = jnp.zeros((tokens, extra), jnp.bfloat16)
    ctx = [None] * tile_count
    cut = 2 * LANES
    ctx_moves = [
        exchange(chunk_count, send_ctx, got_ctx, 0, cut),
        exchange(chunk_count + 1, send_ctx, got_ctx, cut, wide),
    ]
    pair_count = HEADS // 2

    def probabilities(queries, key_rows, bias, pairs):
        scores = []
        for pair in pairs:
            first, last = pair_window(pair)
            scores.append(dot_nt(two_heads(key_rows, pair), queries[:, first:last]))
        return [
            softmax_keys(block * scaling + bias[pair], tokens) for pair, block in zip(pairs, scores)
        ]

    groups = [range(place, place + 2) for place in range(0, pair_count, 2)]
    whole_group = [range(pair_count)]
    for group in groups:
        probs = probabilities(q_time, k_time, bias_wide, group)
        for pair, block in zip(group, probs):
            probs_time[pair] = block
            add_tiles(
                ctx,
                pair_window(pair)[0],
                dot_tn(block.astype(jnp.bfloat16), two_heads(v_time, pair)),
            )
        if group is groups[0]:
            send_ctx[:, :, :cut] = split(jnp.concatenate(ctx[: cut // LANES], axis=1))
            ctx_moves[0][0]()
    send_ctx[:, :, cut:] = split(jnp.concatenate(ctx[cut // LANES :], axis=1))
    ctx_moves[1][0]()
    weight_ready(2)
    weight_ready(3)
    weight_ready(4)
    gain = gain_row(gain_space_ref)
    fold_in[:wide, :] = (out_time[...].astype(jnp.float32) * gain).astype(jnp.bfloat16)
    fold_in[wide:, :] = (hidden[...] * gain).astype(jnp.bfloat16)
    for low, high in cuts:
        block = dot_nn(fold_in[...], proj_space[:, low:high])
        fold[:, low:high] = block[:wide].astype(jnp.bfloat16)
        base[:, low:high] = block[wide:]
    turn(fold, fold_t)
    turn(out_time, out_time_t)
    cot_ctx = dot_nn(cot_ref[...], out_time_t[...])
    for head in range(HEADS):
        row = head % 2 * tokens
        bias_turned[head // 2, row : row + tokens, :] = bias_space[head].T
    ctx_moves[0][1]()
    block = merged(got_ctx, 0, cut).astype(jnp.bfloat16)
    first_part = hidden[...] + dot_nn(block, out_time[:cut])
    sums = add([base[:, low:high] for low, high in cuts], project(block, fold.at[:cut]))
    ctx_moves[1][1]()
    block = merged(got_ctx, cut, wide).astype(jnp.bfloat16)
    after_value = first_part + dot_nn(block, out_time[cut:])
    after[...] = after_value
    inv_space = lax.rsqrt(jnp.mean(after_value * after_value, axis=-1, keepdims=True) + epsilon)
    sums = add(sums, project(block, fold.at[cut:]))
    queries, key_rows, values = by_heads([inv_space * part for part in sums])
    values = jnp.concatenate([values, jnp.zeros((tokens, extra), jnp.bfloat16)], axis=1)
    parts = []
    for group in whole_group:
        probs = probabilities(queries, key_rows, bias_turned, group)
        parts.append(back(queries, key_rows, dc_space, values, probs, group))
    after_ctx = dot_nn(after[...].astype(jnp.bfloat16), out_time_t[...])
    grads = grads_of(parts)
    stack_grads(*grads)
    lean = weighted_sum(grads, (queries, key_rows, values)) * (inv_space * inv_space / width)
    rest_ctx = cot_ctx - lean * after_ctx
    dc_moves = [
        exchange(chunk_count + 2, send_dc, got_dc, 0, cut),
        exchange(chunk_count + 3, send_dc, got_dc, cut, wide),
    ]
    send_dc[:, :, :cut] = split(
        rest_ctx[:, :cut] + inv_space * dot_nn(stacked[...], fold_t[:, :cut])
    )
    dc_moves[0][0]()
    grad_ctx = rest_ctx[:, cut:] + inv_space * dot_nn(stacked[...], fold_t[:, cut:])
    lane = lax.broadcasted_iota(jnp.int32, (1, wide - cut), 1) + cut
    high = inv_time.astype(jnp.bfloat16).astype(jnp.float32)
    spare = jnp.where(lane < HEADS * HD + extra // 2, high, inv_time - high)
    send_dc[:, :, cut:] = split(jnp.where(lane < HEADS * HD, grad_ctx, spare))
    dc_moves[1][0]()
    turn(proj_space, proj_space_t)
    grad_normed = dot_nn(stacked[...], proj_space_t[...])
    grad_after = (
        cot_ref[...].astype(jnp.float32) + inv_space * (grad_normed * gain) - lean * after[...]
    )
    after[...] = grad_after
    after_send[...] = after[pl.ds(pl.multiple_of(other * half, half), half), :].astype(jnp.bfloat16)

    def pair_copy(place, source, target):
        return pltpu.make_async_remote_copy(
            src_ref=source,
            dst_ref=target,
            send_sem=pair_send_sems.at[place],
            recv_sem=pair_recv_sems.at[place],
            device_id=(me, other),
            device_id_type=pl.DeviceIdType.MESH,
        )

    after_copy = pair_copy(0, after_send, after_got)
    after_copy.start()

    turn(proj_time, proj_time_t)
    dc_moves[0][1]()
    dc_time[:, :cut] = merged(got_dc, 0, cut).astype(jnp.bfloat16)
    dc_moves[1][1]()
    rest = merged(got_dc, cut, wide)
    place = HEADS * HD - cut
    inv_rows = rest[:, place : place + 1] + rest[:, wide - cut - 1 :]
    dc_time[:, cut:] = rest.astype(jnp.bfloat16)
    parts = []
    for group in whole_group:
        probs = [probs_time[pair] for pair in group]
        parts.append(back(q_time, k_time, dc_time, v_time, probs, group))
    grads = grads_of(parts)
    stack_grads(*grads)
    lean = weighted_sum(grads, (q_time, k_time, v_time)) * (1.0 / width)
    gain = gain_row(gain_time_ref)
    inverse = 1.0 / gain
    total_copies = []
    for place in range(chunk_count):
        low, high = feature_cuts[place], feature_cuts[place + 1]
        columns = pl.ds(low, high - low)
        grad_normed = dot_nn(stacked[...], proj_time_t[:, low:high])
        tilt = merged(got_normed, low, high) * inverse[:, low:high] * lean
        total = inv_rows * (grad_normed * gain[:, low:high] - tilt)
        totals[:, :, low:high] = total.reshape(seq_count, rows, high - low)
        mine = totals.at[pl.ds(core * half_blocks, half_blocks)]
        pair_send[:, :, low:high] = mine[:, :, low:high].astype(jnp.bfloat16)
        total_copies.append(
            pair_copy(1 + place, pair_send.at[:, :, columns], pair_got.at[:, :, columns])
        )
        total_copies[-1].start()
    my_slot = lax.rem(me, half_blocks)
    my_half = me // half_blocks

    def back_copy(place, slot, source, target, to):
        return pltpu.make_async_remote_copy(
            src_ref=source,
            dst_ref=target,
            send_sem=back_sems.at[0, place],
            recv_sem=back_sems.at[1, place],
            device_id=to,
            device_id_type=pl.DeviceIdType.MESH,
        )

    whole_backs = []
    for place in range(chunk_count):
        low, high = feature_cuts[place], feature_cuts[place + 1]
        columns = pl.ds(low, high - low)
        total_copies[place].wait_recv()
        kept = totals.at[pl.ds(other * half_blocks, half_blocks)]
        send_back[:, :, low:high] = (
            kept[:, :, low:high] + pair_got[:, :, low:high].astype(jnp.float32)
        ).astype(jnp.bfloat16)
        for slot in range(half_blocks):
            back_copy(
                place,
                slot,
                send_back.at[slot, :, columns],
                got_back.at[my_slot, :, columns],
                (other * half_blocks + slot, my_half),
            ).start()
        whole_backs.append(
            back_copy(place, 0, send_back.at[:, :, columns], got_back.at[:, :, columns], (me, other))
        )
    after_copy.wait_recv()
    for place in range(chunk_count):
        low, high = feature_cuts[place], feature_cuts[place + 1]
        whole_backs[place].wait_recv()
        out_ref[:, low:high] = (
            after[pl.ds(pl.multiple_of(core * half, half), half), low:high]
            + after_got[:, low:high].astype(jnp.float32)
            + got_back[:, :, low:high].astype(jnp.float32).reshape(half, high - low)
        )
    for copy in whole_backs:
        copy.wait_send()
    for _, _, finish in (*normed_moves, *ctx_moves, *dc_moves):
        finish()
    for copy in (*pair_copies, after_copy, *total_copies):
        copy.wait_send()


def fused_device(
    clip,
    offsets,
    cotangent,
    gain_time,
    gain_space,
    proj_time,
    out_time,
    proj_space,
    out_space,
    bias_time,
    bias_space,
):
    seq_count = lax.axis_size("seq")
    tokens, width = clip.shape[1:]
    rows = tokens // seq_count
    head_cols = HEADS * HD
    wide = -(-head_cols // LANES) * LANES
    half, half_blocks = tokens // 2, seq_count // 2
    moves = 6
    f32, bf16 = jnp.float32, jnp.bfloat16
    vmem = pltpu.VMEM
    dma = pltpu.SemaphoreType.DMA
    scratch = [
        vmem((tokens, width), bf16),
        vmem((tokens, width), bf16),
        vmem((tokens, width), bf16),
        vmem((width // LANES, LANES), f32),
        vmem((width // LANES, LANES), f32),
        vmem((HEADS * seq_count, seq_count), f32),
        vmem((3 * head_cols, width), bf16),
        vmem((width, wide), bf16),
        vmem((3 * head_cols, width), bf16),
        vmem((width, 3 * head_cols), bf16),
        vmem((wide, width), bf16),
        vmem((width, 3 * head_cols), bf16),
        vmem((wide, width), bf16),
        vmem((HEADS, tokens, tokens), f32),
        vmem((HEADS // 2, 2 * tokens, tokens), f32),
        vmem((HEADS // 2, 2 * tokens, tokens), f32),
        vmem((wide + tokens, width), bf16),
        vmem((wide, 3 * head_cols), bf16),
        vmem((3 * head_cols, wide), bf16),
        vmem((tokens, 3 * head_cols), f32),
        vmem((tokens, width), f32),
        vmem((tokens, width), f32),
        vmem((tokens, wide), bf16),
        vmem((tokens, wide), bf16),
        vmem((tokens, wide), bf16),
        vmem((HEADS // 2, 2 * tokens, tokens), f32),
        vmem((tokens, 3 * head_cols), bf16),
        vmem((tokens, wide), bf16),
        vmem((tokens, wide), bf16),
        vmem((seq_count, rows, width), bf16),
        vmem((seq_count, rows, width), bf16),
        vmem((seq_count, rows, wide), bf16),
        vmem((seq_count, rows, wide), bf16),
        vmem((seq_count, rows, wide), bf16),
        vmem((seq_count, rows, wide), bf16),
        vmem((seq_count, rows, width), f32),
        vmem((half_blocks, rows, width), bf16),
        vmem((half_blocks, rows, width), bf16),
        vmem((half_blocks, rows, width), bf16),
        vmem((half_blocks, rows, width), bf16),
        vmem((half, width), bf16),
        vmem((half, width), bf16),
        dma((moves,)),
        dma((moves,)),
        dma((2, 2)),
        dma((5,)),
        dma((5,)),
        dma((5,)),
        dma((3,)),
        dma((3,)),
        dma((6,)),
    ]
    out_vmem = pl.BlockSpec(memory_space=pltpu.VMEM)
    anywhere = pl.BlockSpec(memory_space=pl.ANY)
    out = pl.pallas_call(
        functools.partial(fused_kernel, seq_count),
        out_shape=pltpu.VMEM((half, width), f32),
        in_specs=[anywhere] * 11,
        out_specs=out_vmem,
        scratch_shapes=scratch,
        compiler_params=pltpu.CompilerParams(
            collective_id=0, has_side_effects=True, vmem_limit_bytes=56 * 1024 * 1024
        ),
    )(
        clip[0],
        offsets[0, 0],
        cotangent[0, 0],
        gain_time.reshape(-1, LANES),
        gain_space.reshape(-1, LANES),
        bias_time.reshape(HEADS * bias_time.shape[1], bias_time.shape[2]),
        proj_time,
        out_time,
        proj_space,
        out_space,
        bias_space,
    )
    return out[None]


def on_device(clip, *rest):
    seq_count = lax.axis_size("seq")
    tokens = clip.shape[1]
    fits = (
        lax.axis_size("dp") == 2
        and clip.shape[0] == 1
        and seq_count & (seq_count - 1) == 0
        and tokens == 8 * seq_count
        and tokens == LANES
        and clip.shape[2] % LANES == 0
    )
    return (fused_device if fits else per_device)(clip, *rest)


def solution(mesh):
    in_specs = (
        P("seq", None, None),
        P("dp", "seq", None, None),
        P("dp", "seq", None, None),
        P(),
        P(),
        P("dp", None),
        P("dp", None),
        P("dp", None),
        P("dp", None),
        P(),
        P(None, "dp", None),
    )
    out_specs = P("seq", "dp", None)
    return jax.shard_map(
        on_device, mesh=mesh, in_specs=in_specs, out_specs=out_specs, check_vma=False
    )
```

```python
import functools
import math

import jax
import jax.numpy as jnp
from jax import lax
from jax.experimental import pallas as pl
from jax.experimental.pallas import tpu as pltpu
from jax.sharding import PartitionSpec as P

HEADS = 8
HD = 72


epsilon = 1e-06


def rms_norm(hidden_in, gain_vec):
    inv_rms = lax.rsqrt(jnp.mean(hidden_in * hidden_in, axis=-1, keepdims=True) + epsilon)
    return ((hidden_in * inv_rms * gain_vec).astype(jnp.bfloat16), inv_rms)


def norm_back(hidden_in, inv_rms, gain_vec, grad_normed):
    weighted = grad_normed.astype(jnp.float32) * gain_vec
    cubed = inv_rms * inv_rms * inv_rms
    return inv_rms * weighted - hidden_in * cubed * jnp.mean(
        weighted * hidden_in, axis=-1, keepdims=True
    )


def layout_forms(frame_major):
    if frame_major:
        return ("lbhe", "mbhe")
    return ("blhe", "bmhe")


def attend(queries, key_rows, values, score_bias, frame_major):
    query_form, key_form = layout_forms(frame_major)
    scaling = 1.0 / math.sqrt(queries.shape[-1])
    scores = (
        jnp.einsum(
            query_form + "," + key_form + "->bhlm",
            queries,
            key_rows,
            preferred_element_type=jnp.float32,
        )
        * scaling
        + score_bias
    )
    highest = jnp.max(scores, axis=-1, keepdims=True)
    exp_scores = jnp.exp(scores - highest)
    probabilities = exp_scores / jnp.sum(exp_scores, axis=-1, keepdims=True)
    context = jnp.einsum(
        "bhlm," + key_form + "->" + query_form,
        probabilities.astype(jnp.bfloat16),
        values,
        preferred_element_type=jnp.float32,
    )
    return (context.astype(jnp.bfloat16), probabilities)


def attend_back(queries, key_rows, values, probabilities, grad_context, frame_major):
    query_form, key_form = layout_forms(frame_major)
    scaling = 1.0 / math.sqrt(queries.shape[-1])
    rounded = probabilities.astype(jnp.bfloat16)
    grad_values = jnp.einsum(
        "bhlm," + query_form + "->" + key_form,
        rounded,
        grad_context,
        preferred_element_type=jnp.float32,
    ).astype(jnp.bfloat16)
    grad_probs = jnp.einsum(
        query_form + "," + key_form + "->bhlm",
        grad_context,
        values,
        preferred_element_type=jnp.float32,
    )
    row_sums = jnp.sum(grad_probs * probabilities, axis=-1, keepdims=True)
    grad_scores = (probabilities * (grad_probs - row_sums) * scaling).astype(jnp.bfloat16)
    grad_queries = jnp.einsum(
        "bhlm," + key_form + "->" + query_form,
        grad_scores,
        key_rows,
        preferred_element_type=jnp.float32,
    ).astype(jnp.bfloat16)
    grad_keys = jnp.einsum(
        "bhlm," + query_form + "->" + key_form,
        grad_scores,
        queries,
        preferred_element_type=jnp.float32,
    ).astype(jnp.bfloat16)
    return (grad_queries, grad_keys, grad_values)


def times_transposed(left, weight):
    return lax.dot_general(
        left, weight, (((1,), (1,)), ((), ())), preferred_element_type=jnp.float32
    )


def regroup(arranged):
    return lax.all_to_all(arranged, "seq", split_axis=0, concat_axis=1, tiled=True)


def to_positions(matrix, stack_count):
    seq_count = lax.axis_size("seq")
    local_rows = matrix.shape[0] // seq_count
    col_count = matrix.shape[1] // stack_count
    arranged = matrix.reshape(seq_count, 1, local_rows, stack_count, col_count)
    return regroup(arranged)[0]


def to_frames(arranged):
    seq_count = lax.axis_size("seq")
    frame_count, local_rows, stack_count, col_count = arranged.shape
    returned = regroup(arranged.reshape(frame_count, 1, local_rows, stack_count, col_count))
    return returned.reshape(seq_count * local_rows, stack_count * col_count)


def per_device(
    clip,
    offsets,
    cotangent,
    gain_time,
    gain_space,
    proj_time,
    out_time,
    proj_space,
    out_space,
    bias_time,
    bias_space,
):
    proj_time, out_time, proj_space, out_space = (
        lax.all_gather(proj_time, "dp", axis=0, tiled=True),
        lax.all_gather(out_time, "dp", axis=0, tiled=True),
        lax.all_gather(proj_space, "dp", axis=0, tiled=True),
        lax.all_gather(out_space, "dp", axis=0, tiled=True),
    )
    bias_space = lax.all_gather(bias_space, "dp", axis=1, tiled=True)
    seq_count = lax.axis_size("seq")
    pos_count = clip.shape[1]
    local_rows = pos_count // seq_count
    head_cols = HEADS * HD
    hidden_in = clip[0].astype(jnp.float32) + offsets[0, 0].astype(jnp.float32)
    normed, inv_rms = rms_norm(hidden_in, gain_time)
    arranged_in = to_positions(normed, 1)
    flat_in = arranged_in.reshape(seq_count * local_rows, arranged_in.shape[-1])
    arranged = jnp.dot(flat_in, proj_time, preferred_element_type=jnp.float32).astype(jnp.bfloat16)
    arranged = arranged.reshape(seq_count, local_rows, 3, HEADS, HD)
    queries, key_rows, values = (arranged[:, :, 0], arranged[:, :, 1], arranged[:, :, 2])
    context, weights_time = attend(queries, key_rows, values, bias_time, True)
    context_frames = to_frames(context.reshape(seq_count, local_rows, 1, head_cols))
    after_time = hidden_in + jnp.dot(context_frames, out_time, preferred_element_type=jnp.float32)
    normed_space, inv_rms_space = rms_norm(after_time, gain_space)
    stacked_space = jnp.dot(normed_space, proj_space, preferred_element_type=jnp.float32).astype(
        jnp.bfloat16
    )
    stacked_space = stacked_space.reshape(1, pos_count, 3, HEADS, HD)
    queries_space, keys_space, values_space = (
        stacked_space[:, :, 0],
        stacked_space[:, :, 1],
        stacked_space[:, :, 2],
    )
    unused_context, weights_space = attend(
        queries_space, keys_space, values_space, bias_space, False
    )
    grad_out = cotangent[0, 0]
    grad_context = (
        times_transposed(grad_out, out_space).astype(jnp.bfloat16).reshape(1, pos_count, HEADS, HD)
    )
    grads_space = attend_back(
        queries_space, keys_space, values_space, weights_space, grad_context, False
    )
    grad_normed = times_transposed(
        jnp.stack(grads_space, axis=2).reshape(pos_count, 3 * head_cols), proj_space
    ).astype(jnp.bfloat16)
    grad_after = grad_out.astype(jnp.float32) + norm_back(
        after_time, inv_rms_space, gain_space, grad_normed
    )
    grad_context_time = times_transposed(grad_after.astype(jnp.bfloat16), out_time).astype(
        jnp.bfloat16
    )
    grad_context_pos = to_positions(grad_context_time, 1).reshape(seq_count, local_rows, HEADS, HD)
    grads_time = attend_back(queries, key_rows, values, weights_time, grad_context_pos, True)
    stacked_grads = jnp.stack(grads_time, axis=2)
    grad_pos = times_transposed(
        stacked_grads.reshape(seq_count * local_rows, 3 * head_cols), proj_time
    ).astype(jnp.bfloat16)
    grad_normed_time = to_frames(grad_pos.reshape(seq_count, local_rows, 1, grad_pos.shape[-1]))
    grad_in = grad_after + norm_back(hidden_in, inv_rms, gain_time, grad_normed_time)
    summed = lax.psum_scatter(
        grad_in.astype(jnp.bfloat16), "dp", scatter_dimension=0, tiled=True
    ).astype(jnp.float32)
    return summed[None]


LANES = 128
MASKED = -1e30


def dot_nn(left, right):
    return lax.dot_general(left, right, (((1,), (0,)), ((), ())), preferred_element_type=jnp.float32)


def dot_nt(left, right):
    return lax.dot_general(left, right, (((1,), (1,)), ((), ())), preferred_element_type=jnp.float32)


def dot_tn(left, right):
    return lax.dot_general(left, right, (((0,), (0,)), ((), ())), preferred_element_type=jnp.float32)


def pair_window(pair):
    first = 2 * pair * HD // LANES * LANES
    last = -(-2 * (pair + 1) * HD // LANES) * LANES
    return first, last


def head_lanes(head, first, last):
    lane = lax.broadcasted_iota(jnp.int32, (1, last - first), 1) + first
    return (lane >= head * HD) & (lane < (head + 1) * HD)


def two_heads(block, pair):
    first, last = pair_window(pair)
    piece = block[:, first:last]
    rows = [
        jnp.where(head_lanes(head, first, last), piece, jnp.zeros_like(piece))
        for head in (2 * pair, 2 * pair + 1)
    ]
    return jnp.concatenate(rows, axis=0)


def add_tiles(tiles, first, block):
    for col in range(0, block.shape[1], LANES):
        tile = (first + col) // LANES
        piece = block[:, col : col + LANES]
        tiles[tile] = piece if tiles[tile] is None else tiles[tile] + piece


def pick_tiles(blocks, tokens, tile_count):
    tiles = []
    for tile in range(tile_count):
        low, high = tile * LANES, (tile + 1) * LANES
        value = jnp.zeros((tokens, LANES), jnp.float32)
        for head in range(HEADS):
            if head * HD < high and (head + 1) * HD > low:
                first, _ = pair_window(head // 2)
                row = head % 2 * tokens
                piece = blocks[head // 2][row : row + tokens, low - first : high - first]
                value = jnp.where(head_lanes(head, low, high), piece, value)
        tiles.append(value)
    return tiles


def softmax_keys(scores, tokens):
    halves = []
    for row in range(0, scores.shape[0], tokens):
        block = scores[row : row + tokens]
        exp_block = jnp.exp(block - jnp.max(block, axis=0, keepdims=True))
        halves.append(exp_block * (1.0 / jnp.sum(exp_block, axis=0, keepdims=True)))
    return jnp.concatenate(halves, axis=0)


def score_grads(grad_probs, probs, tokens, scaling):
    halves = []
    for row in range(0, probs.shape[0], tokens):
        weights, grads = probs[row : row + tokens], grad_probs[row : row + tokens]
        mean = jnp.sum(grads * weights, axis=0, keepdims=True)
        halves.append((weights * (grads - mean) * scaling).astype(jnp.bfloat16))
    return jnp.concatenate(halves, axis=0)


def fused_kernel(
    seq_count,
    clip_in,
    off_in,
    cot_in,
    gain_time_in,
    gain_space_in,
    bias_time_in,
    proj_time_in,
    out_time_in,
    proj_space_in,
    out_space_in,
    bias_space_in,
    out_ref,
    clip_ref,
    off_ref,
    cot_ref,
    gain_time_ref,
    gain_space_ref,
    bias_time_ref,
    proj_time_t,
    out_time_t,
    proj_space_t,
    proj_time,
    out_time,
    proj_space,
    out_space,
    bias_space,
    bias_turned,
    bias_wide,
    fold_in,
    fold,
    fold_t,
    base,
    hidden,
    after,
    q_time,
    k_time,
    v_time,
    probs_time,
    stacked,
    dc_space,
    dc_time,
    send_normed,
    got_normed,
    send_ctx,
    got_ctx,
    send_dc,
    got_dc,
    spare_rows,
    send_back,
    got_back,
    after_send,
    after_got,
    send_sems,
    recv_sems,
    back_sems,
    weight_sems,
    weight_send_sems,
    weight_recv_sems,
    pair_send_sems,
    pair_recv_sems,
    input_sems,
):
    me = lax.axis_index("seq")
    core = lax.axis_index("dp")
    other = 1 - core
    tokens, width = hidden.shape
    rows = tokens // seq_count
    half = tokens // 2
    half_blocks = seq_count // 2
    phases = spare_rows.shape[0] - 1
    wide = q_time.shape[1]
    scaling = 1.0 / math.sqrt(HD)

    barrier = pltpu.get_barrier_semaphore()
    for step in range(seq_count):
        peer = lax.rem(me + step, seq_count)
        if step:
            pl.semaphore_signal(
                barrier, inc=1, device_id=(peer, core), device_id_type=pl.DeviceIdType.MESH
            )
        pl.semaphore_signal(
            barrier, inc=1, device_id=(peer, other), device_id_type=pl.DeviceIdType.MESH
        )

    inputs = (clip_in, off_in, gain_time_in, cot_in, bias_time_in, gain_space_in)
    places = (clip_ref, off_ref, gain_time_ref, cot_ref, bias_time_ref, gain_space_ref)
    input_copies = [
        pltpu.make_async_copy(source, target, input_sems.at[place])
        for place, (source, target) in enumerate(zip(inputs, places))
    ]
    for copy in input_copies:
        copy.start()

    sources = (out_space_in, proj_time_in, out_time_in, proj_space_in)
    targets = (out_space, proj_time, out_time, proj_space)

    def part(place):
        if place == len(sources):
            count = bias_space_in.shape[1]
            start = pl.multiple_of(core * count, count)
            return bias_space_in, bias_space.at[:, pl.ds(start, count)]
        count = sources[place].shape[0]
        start = pl.multiple_of(core * count, count)
        return sources[place], targets[place].at[pl.ds(start, count)]

    weight_count = len(sources) + 1
    own_copies, pair_copies = [], []
    for place in range(weight_count):
        source, target = part(place)
        own_copies.append(pltpu.make_async_copy(source, target, weight_sems.at[place]))
        pair_copies.append(
            pltpu.make_async_remote_copy(
                src_ref=source,
                dst_ref=target,
                send_sem=weight_send_sems.at[place],
                recv_sem=weight_recv_sems.at[place],
                device_id=(me, other),
                device_id_type=pl.DeviceIdType.MESH,
            )
        )

    def weight_ready(place):
        own_copies[place].wait()
        pair_copies[place].wait_recv()

    def partner(step):
        place, bit = me, 1
        while bit <= step:
            if step & bit:
                place = place + bit * (1 - 2 * (me // bit % 2))
            bit *= 2
        return place

    share_rows = rows // 2

    def share(to):
        return pl.ds(pl.multiple_of(to * share_rows, share_rows), share_rows)

    def stay(source, target, send_sem, recv_sem, phase):
        pltpu.make_async_copy(source, target, recv_sem).start()
        unused = spare_rows.at[phase, pl.ds(0, share_rows), pl.ds(0, source.shape[-1])]
        pltpu.make_async_copy(source, unused, send_sem).start()

    def exchange(phase, sent, got, first, last):
        columns = pl.ds(first, last - first)

        def start():
            for step, cross in [(11, 1), (10, 1), (9, 1), (8, 1), (15, 1), (14, 1), (13, 1), (12, 1), (7, 1), (6, 1), (5, 1), (4, 1), (3, 1), (2, 1), (1, 1), (0, 1), (11, 0), (10, 0), (9, 0), (8, 0), (15, 0), (14, 0), (13, 0), (12, 0), (7, 0), (6, 0), (5, 0), (4, 0), (3, 0), (2, 0), (1, 0)]:
                target, to = partner(step), other if cross else core
                pltpu.make_async_remote_copy(
                    src_ref=sent.at[target, share(to), columns],
                    dst_ref=got.at[me, share(core), columns],
                    send_sem=send_sems.at[phase],
                    recv_sem=recv_sems.at[phase],
                    device_id=(target, to),
                    device_id_type=pl.DeviceIdType.MESH,
                ).start()
            own = sent.at[me, share(core), columns]
            stay(own, got.at[me, share(core), columns], send_sems.at[phase], recv_sems.at[phase], phase)

        def whole():
            return pltpu.make_async_remote_copy(
                src_ref=sent.at[:, :, columns],
                dst_ref=got.at[:, :, columns],
                send_sem=send_sems.at[phase],
                recv_sem=recv_sems.at[phase],
                device_id=(me, other),
                device_id_type=pl.DeviceIdType.MESH,
            )

        def arrive():
            whole().wait_recv()

        def finish():
            whole().wait_send()

        return start, arrive, finish

    def merged(ref, first=0, last=None):
        last = ref.shape[-1] if last is None else last
        block = ref[:, :, first:last].astype(jnp.float32)
        return block.reshape(tokens, last - first)

    def split(value):
        return value.reshape(seq_count, rows, value.shape[-1]).astype(jnp.bfloat16)

    def gain_row(gain_ref):
        pieces = [gain_ref[place : place + 1, :] for place in range(gain_ref.shape[0])]
        return jnp.concatenate(pieces, axis=1)

    def norm(value, gain_ref):
        inv_rms = lax.rsqrt(jnp.mean(value * value, axis=-1, keepdims=True) + epsilon)
        return value * inv_rms * gain_row(gain_ref), inv_rms

    head_cols = HEADS * HD
    whole_cols = head_cols // LANES * LANES
    cuts = ((0, whole_cols), (whole_cols, 2 * head_cols), (2 * head_cols, 3 * head_cols))

    def project(block, weight):
        return [dot_nn(block, weight[:, low:high]) for low, high in cuts]

    def add(sums, terms):
        return [a + b for a, b in zip(sums, terms)]

    def by_heads(sums):
        left, middle, values = sums
        queries = jnp.concatenate([left, middle[:, :LANES]], axis=1)
        key_rows = pltpu.roll(middle, middle.shape[1] - (head_cols - whole_cols), 1)
        return queries.astype(jnp.bfloat16), key_rows.astype(jnp.bfloat16), values.astype(jnp.bfloat16)

    def weighted_sum(grads, stacks):
        total = None
        for tiles, stack in zip(grads, stacks):
            for tile, value in enumerate(tiles):
                term = value * stack[:, tile * LANES : (tile + 1) * LANES].astype(jnp.float32)
                total = term if total is None else total + term
        return jnp.sum(total, axis=-1, keepdims=True)

    def stack_grads(dq, dk, dv):
        whole = whole_cols
        dq = jnp.concatenate(dq, axis=1)
        dk = pltpu.roll(jnp.concatenate(dk, axis=1), head_cols - whole, 1)
        dv = jnp.concatenate(dv, axis=1)
        stacked[:, :whole] = dq[:, :whole].astype(jnp.bfloat16)
        stacked[:, whole : whole + LANES] = (dq[:, whole:] + dk[:, :LANES]).astype(jnp.bfloat16)
        stacked[:, whole + LANES : 2 * head_cols] = dk[:, LANES:].astype(jnp.bfloat16)
        stacked[:, 2 * head_cols :] = dv[:, :head_cols].astype(jnp.bfloat16)

    def back(queries, key_rows, grad_ctx, values, probs, pairs):
        windows = [pair_window(pair) for pair in pairs]
        ctxs = [grad_ctx[:, first:last] for first, last in windows]
        grads = [dot_nt(two_heads(values, pair), ctx) for pair, ctx in zip(pairs, ctxs)]
        dv = [dot_nn(block.astype(jnp.bfloat16), ctx) for block, ctx in zip(probs, ctxs)]
        ds = [score_grads(grad, block, tokens, scaling) for grad, block in zip(grads, probs)]
        dk = [dot_nn(block, queries[:, first:last]) for block, (first, last) in zip(ds, windows)]
        dq = [dot_tn(block, two_heads(key_rows, pair)) for block, pair in zip(ds, pairs)]
        return dq, dk, dv

    def grads_of(parts):
        dq, dk, dv = (sum((part[place] for part in parts), []) for place in range(3))
        tiles = [None] * tile_count
        for pair, block in enumerate(dq):
            add_tiles(tiles, pair_window(pair)[0], block)
        return tiles, pick_tiles(dk, tokens, tile_count), pick_tiles(dv, tokens, tile_count)

    def turn(weight, turned):
        for first in range(0, weight.shape[0], LANES):
            turned[:, first : first + LANES] = weight[first : first + LANES, :].T

    tile_count = wide // LANES

    for copy in input_copies[:3]:
        copy.wait()
    for place in (0, 4, 1, 2, 3):
        own_copies[place].start()
    hidden[...] = clip_ref[...].astype(jnp.float32) + off_ref[...].astype(jnp.float32)
    normed, inv_time = norm(hidden[...], gain_time_ref)
    send_normed[...] = split(normed)
    pl.semaphore_wait(barrier, 2 * seq_count - 1)
    feature_cuts = [0, width]
    chunk_count = len(feature_cuts) - 1
    normed_moves = [
        exchange(place, send_normed, got_normed, feature_cuts[place], feature_cuts[place + 1])
        for place in range(chunk_count)
    ]
    for start, _, _ in normed_moves:
        start()
    for place in (0, 4, 1, 2, 3):
        pair_copies[place].start()

    extra = wide - HEADS * HD
    for ref in (out_time, out_space):
        ref[pl.ds(HEADS * HD, extra), :] = jnp.zeros((extra, width), jnp.bfloat16)
    frame = lax.broadcasted_iota(jnp.int32, (seq_count, tokens), 0)
    column = lax.broadcasted_iota(jnp.int32, (seq_count, tokens), 1)
    spread = jnp.where(column // rows == frame, 1.0, 0.0).astype(jnp.float32)
    same = lax.broadcasted_iota(jnp.int32, (tokens, tokens), 0) % rows == (
        lax.broadcasted_iota(jnp.int32, (tokens, tokens), 1) % rows
    )
    for copy in input_copies[3:]:
        copy.wait()
    for head in range(HEADS):
        block = lax.dot_general(
            bias_time_ref[head * seq_count : (head + 1) * seq_count, :],
            spread,
            (((0,), (0,)), ((), ())),
            precision=lax.Precision.HIGHEST,
            preferred_element_type=jnp.float32,
        )
        block = jnp.broadcast_to(block[:, None, :], (seq_count, rows, tokens))
        row = head % 2 * tokens
        bias_wide[head // 2, row : row + tokens, :] = jnp.where(
            same, block.reshape(tokens, tokens), MASKED
        )

    weight_ready(0)
    dc_space[...] = dot_nt(cot_ref[...], out_space[...]).astype(jnp.bfloat16)

    weight_ready(4)
    for head in range(HEADS):
        row = head % 2 * tokens
        bias_turned[head // 2, row : row + tokens, :] = bias_space[head].T
    weight_ready(1)
    weight_ready(2)
    gain = gain_row(gain_space_ref)
    fold_in[:wide, :] = (out_time[...].astype(jnp.float32) * gain).astype(jnp.bfloat16)
    fold_in[wide:, :] = (hidden[...] * gain).astype(jnp.bfloat16)
    turn(out_time, out_time_t)
    cot_ctx = dot_nn(cot_ref[...], out_time_t[...])

    def arrived(place):
        normed_moves[place][1]()
        return merged(got_normed, feature_cuts[place], feature_cuts[place + 1]).astype(jnp.bfloat16)

    sums = project(arrived(0), proj_time.at[: feature_cuts[1]])
    for place in range(1, chunk_count):
        rows_of = proj_time.at[feature_cuts[place] : feature_cuts[place + 1]]
        sums = add(sums, project(arrived(place), rows_of))
    queries, key_rows, values = by_heads(sums)
    q_time[...] = queries
    k_time[...] = key_rows
    v_time[:, : HEADS * HD] = values
    v_time[:, HEADS * HD :] = jnp.zeros((tokens, extra), jnp.bfloat16)
    ctx = [None] * tile_count
    cut = 2 * LANES
    ctx_move = exchange(chunk_count, send_ctx, got_ctx, 0, wide)
    pair_count = HEADS // 2

    def probabilities(queries, key_rows, bias, pairs):
        scores = []
        for pair in pairs:
            first, last = pair_window(pair)
            scores.append(dot_nt(two_heads(key_rows, pair), queries[:, first:last]))
        return [
            softmax_keys(block * scaling + bias[pair], tokens) for pair, block in zip(pairs, scores)
        ]

    groups = [range(place, place + 2) for place in range(0, pair_count, 2)]
    whole_group = [range(pair_count)]
    for group in whole_group:
        probs = probabilities(q_time, k_time, bias_wide, group)
        for pair, block in zip(group, probs):
            probs_time[pair] = block
            add_tiles(
                ctx,
                pair_window(pair)[0],
                dot_tn(block.astype(jnp.bfloat16), two_heads(v_time, pair)),
            )
    send_ctx[...] = split(jnp.concatenate(ctx, axis=1))
    ctx_move[0]()
    weight_ready(3)
    for low, high in cuts:
        block = dot_nn(fold_in[...], proj_space[:, low:high])
        fold[:, low:high] = block[:wide].astype(jnp.bfloat16)
        base[:, low:high] = block[wide:]
    turn(fold, fold_t)
    ctx_move[1]()
    block = merged(got_ctx).astype(jnp.bfloat16)
    after_value = hidden[...] + dot_nn(block, out_time[...])
    after[...] = after_value
    inv_space = lax.rsqrt(jnp.mean(after_value * after_value, axis=-1, keepdims=True) + epsilon)
    sums = add([base[:, low:high] for low, high in cuts], project(block, fold))
    queries, key_rows, values = by_heads([inv_space * part for part in sums])
    values = jnp.concatenate([values, jnp.zeros((tokens, extra), jnp.bfloat16)], axis=1)
    parts = []
    for group in whole_group:
        probs = probabilities(queries, key_rows, bias_turned, group)
        parts.append(back(queries, key_rows, dc_space, values, probs, group))
    after_ctx = dot_nn(after[...].astype(jnp.bfloat16), out_time_t[...])
    grads = grads_of(parts)
    stack_grads(*grads)
    lean = weighted_sum(grads, (queries, key_rows, values)) * (inv_space * inv_space / width)
    rest_ctx = cot_ctx - lean * after_ctx
    dc_move = exchange(chunk_count + 1, send_dc, got_dc, 0, wide)
    grad_ctx = rest_ctx + inv_space * dot_nn(stacked[...], fold_t[...])
    lane = lax.broadcasted_iota(jnp.int32, (1, wide), 1)
    high = inv_time.astype(jnp.bfloat16).astype(jnp.float32)
    spare = jnp.where(lane < HEADS * HD + extra // 2, high, inv_time - high)
    send_dc[...] = split(jnp.where(lane < HEADS * HD, grad_ctx, spare))
    dc_move[0]()
    turn(proj_space, proj_space_t)
    grad_normed = dot_nn(stacked[...], proj_space_t[...])
    grad_after = (
        cot_ref[...].astype(jnp.float32) + inv_space * (grad_normed * gain) - lean * after[...]
    )
    after[...] = grad_after
    after_send[...] = after[pl.ds(pl.multiple_of(other * half, half), half), :].astype(jnp.bfloat16)

    def pair_copy(place, source, target):
        return pltpu.make_async_remote_copy(
            src_ref=source,
            dst_ref=target,
            send_sem=pair_send_sems.at[place],
            recv_sem=pair_recv_sems.at[place],
            device_id=(me, other),
            device_id_type=pl.DeviceIdType.MESH,
        )

    after_copy = pair_copy(0, after_send, after_got)
    after_copy.start()

    turn(proj_time, proj_time_t)
    dc_move[1]()
    block = merged(got_dc)
    inv_rows = block[:, HEADS * HD : HEADS * HD + 1] + block[:, wide - 1 :]
    dc_time[...] = block.astype(jnp.bfloat16)
    parts = []
    for group in whole_group:
        probs = [probs_time[pair] for pair in group]
        parts.append(back(q_time, k_time, dc_time, v_time, probs, group))
    grads = grads_of(parts)
    stack_grads(*grads)
    lean = weighted_sum(grads, (q_time, k_time, v_time)) * (1.0 / width)
    gain = gain_row(gain_time_ref)
    inverse = 1.0 / gain
    tilt = merged(got_normed) * inverse * lean
    total = inv_rows * (dot_nn(stacked[...], proj_time_t[...]) * gain - tilt)
    total = total + pltpu.roll(total, tokens - share_rows, 0)
    send_back[...] = split(total)
    my_slot = lax.rem(me, half_blocks)
    my_half = me // half_blocks
    send_sem, recv_sem = back_sems.at[0], back_sems.at[1]

    def back_copy(target):
        return pltpu.make_async_remote_copy(
            src_ref=send_back.at[target, pl.ds(0, share_rows)],
            dst_ref=got_back.at[my_slot, share(core)],
            send_sem=send_sem,
            recv_sem=recv_sem,
            device_id=(target, my_half),
            device_id_type=pl.DeviceIdType.MESH,
        )

    for step in range(seq_count - 1, 0, -1):
        back_copy(partner(step)).start()

    @pl.when(my_half != core)
    def _():
        back_copy(me).start()

    @pl.when(my_half == core)
    def _():
        source = send_back.at[me, pl.ds(0, share_rows)]
        stay(source, got_back.at[my_slot, share(core)], send_sem, recv_sem, phases)

    whole_back = pltpu.make_async_remote_copy(
        src_ref=send_back.at[pl.ds(0, half_blocks)],
        dst_ref=got_back,
        send_sem=send_sem,
        recv_sem=recv_sem,
        device_id=(me, other),
        device_id_type=pl.DeviceIdType.MESH,
    )
    after_copy.wait_recv()
    whole_back.wait_recv()
    out_ref[...] = (
        after[pl.ds(pl.multiple_of(core * half, half), half), :]
        + after_got[...].astype(jnp.float32)
        + got_back[...].astype(jnp.float32).reshape(half, width)
    )
    whole_back.wait_send()
    for _, _, finish in (*normed_moves, ctx_move, dc_move):
        finish()
    for copy in (*pair_copies, after_copy):
        copy.wait_send()


def fused_device(
    clip,
    offsets,
    cotangent,
    gain_time,
    gain_space,
    proj_time,
    out_time,
    proj_space,
    out_space,
    bias_time,
    bias_space,
):
    seq_count = lax.axis_size("seq")
    tokens, width = clip.shape[1:]
    rows = tokens // seq_count
    head_cols = HEADS * HD
    wide = -(-head_cols // LANES) * LANES
    half, half_blocks = tokens // 2, seq_count // 2
    moves = 3
    f32, bf16 = jnp.float32, jnp.bfloat16
    vmem = pltpu.VMEM
    dma = pltpu.SemaphoreType.DMA
    scratch = [
        vmem((tokens, width), bf16),
        vmem((tokens, width), bf16),
        vmem((tokens, width), bf16),
        vmem((width // LANES, LANES), f32),
        vmem((width // LANES, LANES), f32),
        vmem((HEADS * seq_count, seq_count), f32),
        vmem((3 * head_cols, width), bf16),
        vmem((width, wide), bf16),
        vmem((3 * head_cols, width), bf16),
        vmem((width, 3 * head_cols), bf16),
        vmem((wide, width), bf16),
        vmem((width, 3 * head_cols), bf16),
        vmem((wide, width), bf16),
        vmem((HEADS, tokens, tokens), f32),
        vmem((HEADS // 2, 2 * tokens, tokens), f32),
        vmem((HEADS // 2, 2 * tokens, tokens), f32),
        vmem((wide + tokens, width), bf16),
        vmem((wide, 3 * head_cols), bf16),
        vmem((3 * head_cols, wide), bf16),
        vmem((tokens, 3 * head_cols), f32),
        vmem((tokens, width), f32),
        vmem((tokens, width), f32),
        vmem((tokens, wide), bf16),
        vmem((tokens, wide), bf16),
        vmem((tokens, wide), bf16),
        vmem((HEADS // 2, 2 * tokens, tokens), f32),
        vmem((tokens, 3 * head_cols), bf16),
        vmem((tokens, wide), bf16),
        vmem((tokens, wide), bf16),
        vmem((seq_count, rows, width), bf16),
        vmem((seq_count, rows, width), bf16),
        vmem((seq_count, rows, wide), bf16),
        vmem((seq_count, rows, wide), bf16),
        vmem((seq_count, rows, wide), bf16),
        vmem((seq_count, rows, wide), bf16),
        vmem((moves + 1, rows, width), bf16),
        vmem((seq_count, rows, width), bf16),
        vmem((half_blocks, rows, width), bf16),
        vmem((half, width), bf16),
        vmem((half, width), bf16),
        dma((moves,)),
        dma((moves,)),
        dma((2,)),
        dma((5,)),
        dma((5,)),
        dma((5,)),
        dma((1,)),
        dma((1,)),
        dma((6,)),
    ]
    out_vmem = pl.BlockSpec(memory_space=pltpu.VMEM)
    anywhere = pl.BlockSpec(memory_space=pl.ANY)
    out = pl.pallas_call(
        functools.partial(fused_kernel, seq_count),
        out_shape=pltpu.VMEM((half, width), f32),
        in_specs=[anywhere] * 11,
        out_specs=out_vmem,
        scratch_shapes=scratch,
        compiler_params=pltpu.CompilerParams(
            collective_id=0, has_side_effects=True, vmem_limit_bytes=56 * 1024 * 1024
        ),
    )(
        clip[0],
        offsets[0, 0],
        cotangent[0, 0],
        gain_time.reshape(-1, LANES),
        gain_space.reshape(-1, LANES),
        bias_time.reshape(HEADS * bias_time.shape[1], bias_time.shape[2]),
        proj_time,
        out_time,
        proj_space,
        out_space,
        bias_space,
    )
    return out[None]


def on_device(clip, *rest):
    seq_count = lax.axis_size("seq")
    tokens = clip.shape[1]
    fits = (
        lax.axis_size("dp") == 2
        and clip.shape[0] == 1
        and seq_count & (seq_count - 1) == 0
        and tokens == 8 * seq_count
        and tokens == LANES
        and clip.shape[2] % LANES == 0
    )
    return (fused_device if fits else per_device)(clip, *rest)


def solution(mesh):
    in_specs = (
        P("seq", None, None),
        P("dp", "seq", None, None),
        P("dp", "seq", None, None),
        P(),
        P(),
        P("dp", None),
        P("dp", None),
        P("dp", None),
        P("dp", None),
        P(),
        P(None, "dp", None),
    )
    out_specs = P("seq", "dp", None)
    return jax.shard_map(
        on_device, mesh=mesh, in_specs=in_specs, out_specs=out_specs, check_vma=False
    )
```

```python
import functools
import math

import jax
import jax.numpy as jnp
from jax import lax
from jax.experimental import pallas as pl
from jax.experimental.pallas import tpu as pltpu
from jax.sharding import PartitionSpec as P

HEADS = 8
HD = 72


epsilon = 1e-06


def rms_norm(hidden_in, gain_vec):
    inv_rms = lax.rsqrt(jnp.mean(hidden_in * hidden_in, axis=-1, keepdims=True) + epsilon)
    return ((hidden_in * inv_rms * gain_vec).astype(jnp.bfloat16), inv_rms)


def norm_back(hidden_in, inv_rms, gain_vec, grad_normed):
    weighted = grad_normed.astype(jnp.float32) * gain_vec
    cubed = inv_rms * inv_rms * inv_rms
    return inv_rms * weighted - hidden_in * cubed * jnp.mean(
        weighted * hidden_in, axis=-1, keepdims=True
    )


def layout_forms(frame_major):
    if frame_major:
        return ("lbhe", "mbhe")
    return ("blhe", "bmhe")


def attend(queries, key_rows, values, score_bias, frame_major):
    query_form, key_form = layout_forms(frame_major)
    scaling = 1.0 / math.sqrt(queries.shape[-1])
    scores = (
        jnp.einsum(
            query_form + "," + key_form + "->bhlm",
            queries,
            key_rows,
            preferred_element_type=jnp.float32,
        )
        * scaling
        + score_bias
    )
    highest = jnp.max(scores, axis=-1, keepdims=True)
    exp_scores = jnp.exp(scores - highest)
    probabilities = exp_scores / jnp.sum(exp_scores, axis=-1, keepdims=True)
    context = jnp.einsum(
        "bhlm," + key_form + "->" + query_form,
        probabilities.astype(jnp.bfloat16),
        values,
        preferred_element_type=jnp.float32,
    )
    return (context.astype(jnp.bfloat16), probabilities)


def attend_back(queries, key_rows, values, probabilities, grad_context, frame_major):
    query_form, key_form = layout_forms(frame_major)
    scaling = 1.0 / math.sqrt(queries.shape[-1])
    rounded = probabilities.astype(jnp.bfloat16)
    grad_values = jnp.einsum(
        "bhlm," + query_form + "->" + key_form,
        rounded,
        grad_context,
        preferred_element_type=jnp.float32,
    ).astype(jnp.bfloat16)
    grad_probs = jnp.einsum(
        query_form + "," + key_form + "->bhlm",
        grad_context,
        values,
        preferred_element_type=jnp.float32,
    )
    row_sums = jnp.sum(grad_probs * probabilities, axis=-1, keepdims=True)
    grad_scores = (probabilities * (grad_probs - row_sums) * scaling).astype(jnp.bfloat16)
    grad_queries = jnp.einsum(
        "bhlm," + key_form + "->" + query_form,
        grad_scores,
        key_rows,
        preferred_element_type=jnp.float32,
    ).astype(jnp.bfloat16)
    grad_keys = jnp.einsum(
        "bhlm," + query_form + "->" + key_form,
        grad_scores,
        queries,
        preferred_element_type=jnp.float32,
    ).astype(jnp.bfloat16)
    return (grad_queries, grad_keys, grad_values)


def times_transposed(left, weight):
    return lax.dot_general(
        left, weight, (((1,), (1,)), ((), ())), preferred_element_type=jnp.float32
    )


def regroup(arranged):
    return lax.all_to_all(arranged, "seq", split_axis=0, concat_axis=1, tiled=True)


def to_positions(matrix, stack_count):
    seq_count = lax.axis_size("seq")
    local_rows = matrix.shape[0] // seq_count
    col_count = matrix.shape[1] // stack_count
    arranged = matrix.reshape(seq_count, 1, local_rows, stack_count, col_count)
    return regroup(arranged)[0]


def to_frames(arranged):
    seq_count = lax.axis_size("seq")
    frame_count, local_rows, stack_count, col_count = arranged.shape
    returned = regroup(arranged.reshape(frame_count, 1, local_rows, stack_count, col_count))
    return returned.reshape(seq_count * local_rows, stack_count * col_count)


def per_device(
    clip,
    offsets,
    cotangent,
    gain_time,
    gain_space,
    proj_time,
    out_time,
    proj_space,
    out_space,
    bias_time,
    bias_space,
):
    proj_time, out_time, proj_space, out_space = (
        lax.all_gather(proj_time, "dp", axis=0, tiled=True),
        lax.all_gather(out_time, "dp", axis=0, tiled=True),
        lax.all_gather(proj_space, "dp", axis=0, tiled=True),
        lax.all_gather(out_space, "dp", axis=0, tiled=True),
    )
    bias_space = lax.all_gather(bias_space, "dp", axis=1, tiled=True)
    seq_count = lax.axis_size("seq")
    pos_count = clip.shape[1]
    local_rows = pos_count // seq_count
    head_cols = HEADS * HD
    hidden_in = clip[0].astype(jnp.float32) + offsets[0, 0].astype(jnp.float32)
    normed, inv_rms = rms_norm(hidden_in, gain_time)
    arranged_in = to_positions(normed, 1)
    flat_in = arranged_in.reshape(seq_count * local_rows, arranged_in.shape[-1])
    arranged = jnp.dot(flat_in, proj_time, preferred_element_type=jnp.float32).astype(jnp.bfloat16)
    arranged = arranged.reshape(seq_count, local_rows, 3, HEADS, HD)
    queries, key_rows, values = (arranged[:, :, 0], arranged[:, :, 1], arranged[:, :, 2])
    context, weights_time = attend(queries, key_rows, values, bias_time, True)
    context_frames = to_frames(context.reshape(seq_count, local_rows, 1, head_cols))
    after_time = hidden_in + jnp.dot(context_frames, out_time, preferred_element_type=jnp.float32)
    normed_space, inv_rms_space = rms_norm(after_time, gain_space)
    stacked_space = jnp.dot(normed_space, proj_space, preferred_element_type=jnp.float32).astype(
        jnp.bfloat16
    )
    stacked_space = stacked_space.reshape(1, pos_count, 3, HEADS, HD)
    queries_space, keys_space, values_space = (
        stacked_space[:, :, 0],
        stacked_space[:, :, 1],
        stacked_space[:, :, 2],
    )
    unused_context, weights_space = attend(
        queries_space, keys_space, values_space, bias_space, False
    )
    grad_out = cotangent[0, 0]
    grad_context = (
        times_transposed(grad_out, out_space).astype(jnp.bfloat16).reshape(1, pos_count, HEADS, HD)
    )
    grads_space = attend_back(
        queries_space, keys_space, values_space, weights_space, grad_context, False
    )
    grad_normed = times_transposed(
        jnp.stack(grads_space, axis=2).reshape(pos_count, 3 * head_cols), proj_space
    ).astype(jnp.bfloat16)
    grad_after = grad_out.astype(jnp.float32) + norm_back(
        after_time, inv_rms_space, gain_space, grad_normed
    )
    grad_context_time = times_transposed(grad_after.astype(jnp.bfloat16), out_time).astype(
        jnp.bfloat16
    )
    grad_context_pos = to_positions(grad_context_time, 1).reshape(seq_count, local_rows, HEADS, HD)
    grads_time = attend_back(queries, key_rows, values, weights_time, grad_context_pos, True)
    stacked_grads = jnp.stack(grads_time, axis=2)
    grad_pos = times_transposed(
        stacked_grads.reshape(seq_count * local_rows, 3 * head_cols), proj_time
    ).astype(jnp.bfloat16)
    grad_normed_time = to_frames(grad_pos.reshape(seq_count, local_rows, 1, grad_pos.shape[-1]))
    grad_in = grad_after + norm_back(hidden_in, inv_rms, gain_time, grad_normed_time)
    summed = lax.psum_scatter(
        grad_in.astype(jnp.bfloat16), "dp", scatter_dimension=0, tiled=True
    ).astype(jnp.float32)
    return summed[None]


LANES = 128
MASKED = -1e30


def dot_nn(left, right):
    return lax.dot_general(left, right, (((1,), (0,)), ((), ())), preferred_element_type=jnp.float32)


def dot_nt(left, right):
    return lax.dot_general(left, right, (((1,), (1,)), ((), ())), preferred_element_type=jnp.float32)


def dot_tn(left, right):
    return lax.dot_general(left, right, (((0,), (0,)), ((), ())), preferred_element_type=jnp.float32)


def pair_window(pair):
    first = 2 * pair * HD // LANES * LANES
    last = -(-2 * (pair + 1) * HD // LANES) * LANES
    return first, last


def head_lanes(head, first, last):
    lane = lax.broadcasted_iota(jnp.int32, (1, last - first), 1) + first
    return (lane >= head * HD) & (lane < (head + 1) * HD)


def two_heads(block, pair):
    first, last = pair_window(pair)
    piece = block[:, first:last]
    rows = [
        jnp.where(head_lanes(head, first, last), piece, jnp.zeros_like(piece))
        for head in (2 * pair, 2 * pair + 1)
    ]
    return jnp.concatenate(rows, axis=0)


def add_tiles(tiles, first, block):
    for col in range(0, block.shape[1], LANES):
        tile = (first + col) // LANES
        piece = block[:, col : col + LANES]
        tiles[tile] = piece if tiles[tile] is None else tiles[tile] + piece


def pick_tiles(blocks, tokens, tile_count):
    tiles = []
    for tile in range(tile_count):
        low, high = tile * LANES, (tile + 1) * LANES
        value = jnp.zeros((tokens, LANES), jnp.float32)
        for head in range(HEADS):
            if head * HD < high and (head + 1) * HD > low:
                first, _ = pair_window(head // 2)
                row = head % 2 * tokens
                piece = blocks[head // 2][row : row + tokens, low - first : high - first]
                value = jnp.where(head_lanes(head, low, high), piece, value)
        tiles.append(value)
    return tiles


def softmax_keys(scores, tokens):
    halves = []
    for row in range(0, scores.shape[0], tokens):
        block = scores[row : row + tokens]
        exp_block = jnp.exp(block - jnp.max(block, axis=0, keepdims=True))
        halves.append(exp_block * (1.0 / jnp.sum(exp_block, axis=0, keepdims=True)))
    return jnp.concatenate(halves, axis=0)


def score_grads(grad_probs, probs, tokens, scaling):
    halves = []
    for row in range(0, probs.shape[0], tokens):
        weights, grads = probs[row : row + tokens], grad_probs[row : row + tokens]
        mean = jnp.sum(grads * weights, axis=0, keepdims=True)
        halves.append((weights * (grads - mean) * scaling).astype(jnp.bfloat16))
    return jnp.concatenate(halves, axis=0)


def fused_kernel(
    seq_count,
    clip_in,
    off_in,
    cot_in,
    gain_time_in,
    gain_space_in,
    bias_time_in,
    proj_time_in,
    out_time_in,
    proj_space_in,
    out_space_in,
    bias_space_in,
    out_ref,
    clip_ref,
    off_ref,
    cot_ref,
    gain_time_ref,
    gain_space_ref,
    bias_time_ref,
    proj_time_t,
    out_time_t,
    proj_space_t,
    proj_time,
    out_time,
    proj_space,
    out_space,
    bias_space,
    bias_turned,
    bias_wide,
    fold_in,
    fold,
    fold_t,
    base,
    hidden,
    after,
    q_time,
    k_time,
    v_time,
    probs_time,
    stacked,
    dc_space,
    dc_time,
    send_normed,
    got_normed,
    send_ctx,
    got_ctx,
    send_dc,
    got_dc,
    spare_rows,
    send_back,
    got_back,
    after_send,
    after_got,
    send_sems,
    recv_sems,
    back_sems,
    weight_sems,
    weight_send_sems,
    weight_recv_sems,
    pair_send_sems,
    pair_recv_sems,
    input_sems,
):
    me = lax.axis_index("seq")
    core = lax.axis_index("dp")
    other = 1 - core
    tokens, width = hidden.shape
    rows = tokens // seq_count
    half = tokens // 2
    half_blocks = seq_count // 2
    phases = spare_rows.shape[0] - 1
    wide = q_time.shape[1]
    scaling = 1.0 / math.sqrt(HD)

    barrier = pltpu.get_barrier_semaphore()
    for step in range(seq_count):
        peer = lax.rem(me + step, seq_count)
        if step:
            pl.semaphore_signal(
                barrier, inc=1, device_id=(peer, core), device_id_type=pl.DeviceIdType.MESH
            )
        pl.semaphore_signal(
            barrier, inc=1, device_id=(peer, other), device_id_type=pl.DeviceIdType.MESH
        )

    inputs = (clip_in, off_in, gain_time_in, cot_in, bias_time_in, gain_space_in)
    places = (clip_ref, off_ref, gain_time_ref, cot_ref, bias_time_ref, gain_space_ref)
    input_copies = [
        pltpu.make_async_copy(source, target, input_sems.at[place])
        for place, (source, target) in enumerate(zip(inputs, places))
    ]
    for copy in input_copies:
        copy.start()

    sources = (out_space_in, proj_time_in, out_time_in, proj_space_in)
    targets = (out_space, proj_time, out_time, proj_space)

    def part(place):
        if place == len(sources):
            count = bias_space_in.shape[1]
            start = pl.multiple_of(core * count, count)
            return bias_space_in, bias_space.at[:, pl.ds(start, count)]
        count = sources[place].shape[0]
        start = pl.multiple_of(core * count, count)
        return sources[place], targets[place].at[pl.ds(start, count)]

    weight_count = len(sources) + 1
    own_copies, pair_copies = [], []
    for place in range(weight_count):
        source, target = part(place)
        own_copies.append(pltpu.make_async_copy(source, target, weight_sems.at[place]))
        pair_copies.append(
            pltpu.make_async_remote_copy(
                src_ref=source,
                dst_ref=target,
                send_sem=weight_send_sems.at[place],
                recv_sem=weight_recv_sems.at[place],
                device_id=(me, other),
                device_id_type=pl.DeviceIdType.MESH,
            )
        )

    def weight_ready(place):
        own_copies[place].wait()
        pair_copies[place].wait_recv()

    def partner(step):
        place, bit = me, 1
        while bit <= step:
            if step & bit:
                place = place + bit * (1 - 2 * (me // bit % 2))
            bit *= 2
        return place

    share_rows = rows // 2
    quarter = seq_count // 4
    far = [*range(3 * quarter - 1, 2 * quarter - 1, -1), *range(seq_count - 1, 3 * quarter - 1, -1)]
    steps = [*far, *range(2 * quarter - 1, 0, -1)]

    def share(to):
        return pl.ds(pl.multiple_of(to * share_rows, share_rows), share_rows)

    def stay(source, target, send_sem, recv_sem, phase):
        pltpu.make_async_copy(source, target, recv_sem).start()
        unused = spare_rows.at[phase, pl.ds(0, share_rows), pl.ds(0, source.shape[-1])]
        pltpu.make_async_copy(source, unused, send_sem).start()

    def exchange(phase, sent, got, first, last):
        columns = pl.ds(first, last - first)

        def start():
            for step, to in (*[(step, 1) for step in steps], *[(step, 0) for step in steps], (0, other)):
                target = partner(step)
                pltpu.make_async_remote_copy(
                    src_ref=sent.at[target, share(to), columns],
                    dst_ref=got.at[me, share(core), columns],
                    send_sem=send_sems.at[phase],
                    recv_sem=recv_sems.at[phase],
                    device_id=(target, to),
                    device_id_type=pl.DeviceIdType.MESH,
                ).start()
            own = sent.at[me, share(core), columns]
            stay(own, got.at[me, share(core), columns], send_sems.at[phase], recv_sems.at[phase], phase)

        def whole():
            return pltpu.make_async_remote_copy(
                src_ref=sent.at[:, :, columns],
                dst_ref=got.at[:, :, columns],
                send_sem=send_sems.at[phase],
                recv_sem=recv_sems.at[phase],
                device_id=(me, other),
                device_id_type=pl.DeviceIdType.MESH,
            )

        def arrive():
            whole().wait_recv()

        def finish():
            whole().wait_send()

        return start, arrive, finish

    def merged(ref, first=0, last=None):
        last = ref.shape[-1] if last is None else last
        block = ref[:, :, first:last].astype(jnp.float32)
        return block.reshape(tokens, last - first)

    def split(value):
        return value.reshape(seq_count, rows, value.shape[-1]).astype(jnp.bfloat16)

    def gain_row(gain_ref):
        pieces = [gain_ref[place : place + 1, :] for place in range(gain_ref.shape[0])]
        return jnp.concatenate(pieces, axis=1)

    def norm(value, gain_ref):
        inv_rms = lax.rsqrt(jnp.mean(value * value, axis=-1, keepdims=True) + epsilon)
        return value * inv_rms * gain_row(gain_ref), inv_rms

    head_cols = HEADS * HD
    whole_cols = head_cols // LANES * LANES
    cuts = ((0, whole_cols), (whole_cols, 2 * head_cols), (2 * head_cols, 3 * head_cols))

    def project(block, weight):
        return [dot_nn(block, weight[:, low:high]) for low, high in cuts]

    def add(sums, terms):
        return [a + b for a, b in zip(sums, terms)]

    def by_heads(sums):
        left, middle, values = sums
        queries = jnp.concatenate([left, middle[:, :LANES]], axis=1)
        key_rows = pltpu.roll(middle, middle.shape[1] - (head_cols - whole_cols), 1)
        return queries.astype(jnp.bfloat16), key_rows.astype(jnp.bfloat16), values.astype(jnp.bfloat16)

    def weighted_sum(grads, stacks):
        total = None
        for tiles, stack in zip(grads, stacks):
            for tile, value in enumerate(tiles):
                term = value * stack[:, tile * LANES : (tile + 1) * LANES].astype(jnp.float32)
                total = term if total is None else total + term
        return jnp.sum(total, axis=-1, keepdims=True)

    def stack_grads(dq, dk, dv):
        whole = whole_cols
        dq = jnp.concatenate(dq, axis=1)
        dk = pltpu.roll(jnp.concatenate(dk, axis=1), head_cols - whole, 1)
        dv = jnp.concatenate(dv, axis=1)
        stacked[:, :whole] = dq[:, :whole].astype(jnp.bfloat16)
        stacked[:, whole : whole + LANES] = (dq[:, whole:] + dk[:, :LANES]).astype(jnp.bfloat16)
        stacked[:, whole + LANES : 2 * head_cols] = dk[:, LANES:].astype(jnp.bfloat16)
        stacked[:, 2 * head_cols :] = dv[:, :head_cols].astype(jnp.bfloat16)

    def back(queries, key_rows, grad_ctx, values, probs, pairs):
        windows = [pair_window(pair) for pair in pairs]
        ctxs = [grad_ctx[:, first:last] for first, last in windows]
        grads = [dot_nt(two_heads(values, pair), ctx) for pair, ctx in zip(pairs, ctxs)]
        dv = [dot_nn(block.astype(jnp.bfloat16), ctx) for block, ctx in zip(probs, ctxs)]
        ds = [score_grads(grad, block, tokens, scaling) for grad, block in zip(grads, probs)]
        dk = [dot_nn(block, queries[:, first:last]) for block, (first, last) in zip(ds, windows)]
        dq = [dot_tn(block, two_heads(key_rows, pair)) for block, pair in zip(ds, pairs)]
        return dq, dk, dv

    def grads_of(parts):
        dq, dk, dv = (sum((part[place] for part in parts), []) for place in range(3))
        tiles = [None] * tile_count
        for pair, block in enumerate(dq):
            add_tiles(tiles, pair_window(pair)[0], block)
        return tiles, pick_tiles(dk, tokens, tile_count), pick_tiles(dv, tokens, tile_count)

    def turn(weight, turned):
        for first in range(0, weight.shape[0], LANES):
            turned[:, first : first + LANES] = weight[first : first + LANES, :].T

    tile_count = wide // LANES

    for copy in input_copies[:3]:
        copy.wait()
    for place in (0, 4, 1, 2, 3):
        own_copies[place].start()
    hidden[...] = clip_ref[...].astype(jnp.float32) + off_ref[...].astype(jnp.float32)
    normed, inv_time = norm(hidden[...], gain_time_ref)
    send_normed[...] = split(normed)
    pl.semaphore_wait(barrier, 2 * seq_count - 1)
    feature_cuts = [0, width]
    chunk_count = len(feature_cuts) - 1
    normed_moves = [
        exchange(place, send_normed, got_normed, feature_cuts[place], feature_cuts[place + 1])
        for place in range(chunk_count)
    ]
    for start, _, _ in normed_moves:
        start()
    for place in (0, 4, 1, 2, 3):
        pair_copies[place].start()

    extra = wide - HEADS * HD
    for ref in (out_time, out_space):
        ref[pl.ds(HEADS * HD, extra), :] = jnp.zeros((extra, width), jnp.bfloat16)
    frame = lax.broadcasted_iota(jnp.int32, (seq_count, tokens), 0)
    column = lax.broadcasted_iota(jnp.int32, (seq_count, tokens), 1)
    spread = jnp.where(column // rows == frame, 1.0, 0.0).astype(jnp.float32)
    same = lax.broadcasted_iota(jnp.int32, (tokens, tokens), 0) % rows == (
        lax.broadcasted_iota(jnp.int32, (tokens, tokens), 1) % rows
    )
    for copy in input_copies[3:]:
        copy.wait()
    for head in range(HEADS):
        block = lax.dot_general(
            bias_time_ref[head * seq_count : (head + 1) * seq_count, :],
            spread,
            (((0,), (0,)), ((), ())),
            precision=lax.Precision.HIGHEST,
            preferred_element_type=jnp.float32,
        )
        block = jnp.broadcast_to(block[:, None, :], (seq_count, rows, tokens))
        row = head % 2 * tokens
        bias_wide[head // 2, row : row + tokens, :] = jnp.where(
            same, block.reshape(tokens, tokens), MASKED
        )

    weight_ready(0)
    dc_space[...] = dot_nt(cot_ref[...], out_space[...]).astype(jnp.bfloat16)

    weight_ready(4)
    for head in range(HEADS):
        row = head % 2 * tokens
        bias_turned[head // 2, row : row + tokens, :] = bias_space[head].T
    weight_ready(1)
    weight_ready(2)
    gain = gain_row(gain_space_ref)
    fold_in[:wide, :] = (out_time[...].astype(jnp.float32) * gain).astype(jnp.bfloat16)
    fold_in[wide:, :] = (hidden[...] * gain).astype(jnp.bfloat16)
    turn(out_time, out_time_t)
    cot_ctx = dot_nn(cot_ref[...], out_time_t[...])

    def arrived(place):
        normed_moves[place][1]()
        return merged(got_normed, feature_cuts[place], feature_cuts[place + 1]).astype(jnp.bfloat16)

    sums = project(arrived(0), proj_time.at[: feature_cuts[1]])
    for place in range(1, chunk_count):
        rows_of = proj_time.at[feature_cuts[place] : feature_cuts[place + 1]]
        sums = add(sums, project(arrived(place), rows_of))
    queries, key_rows, values = by_heads(sums)
    q_time[...] = queries
    k_time[...] = key_rows
    v_time[:, : HEADS * HD] = values
    v_time[:, HEADS * HD :] = jnp.zeros((tokens, extra), jnp.bfloat16)
    ctx = [None] * tile_count
    cut = 2 * LANES
    ctx_move = exchange(chunk_count, send_ctx, got_ctx, 0, wide)
    pair_count = HEADS // 2

    def probabilities(queries, key_rows, bias, pairs):
        scores = []
        for pair in pairs:
            first, last = pair_window(pair)
            scores.append(dot_nt(two_heads(key_rows, pair), queries[:, first:last]))
        return [
            softmax_keys(block * scaling + bias[pair], tokens) for pair, block in zip(pairs, scores)
        ]

    groups = [range(place, place + 2) for place in range(0, pair_count, 2)]
    whole_group = [range(pair_count)]
    for group in whole_group:
        probs = probabilities(q_time, k_time, bias_wide, group)
        for pair, block in zip(group, probs):
            probs_time[pair] = block
            add_tiles(
                ctx,
                pair_window(pair)[0],
                dot_tn(block.astype(jnp.bfloat16), two_heads(v_time, pair)),
            )
    send_ctx[...] = split(jnp.concatenate(ctx, axis=1))
    ctx_move[0]()
    weight_ready(3)
    for low, high in cuts:
        block = dot_nn(fold_in[...], proj_space[:, low:high])
        fold[:, low:high] = block[:wide].astype(jnp.bfloat16)
        base[:, low:high] = block[wide:]
    turn(fold, fold_t)
    ctx_move[1]()
    block = merged(got_ctx).astype(jnp.bfloat16)
    after_value = hidden[...] + dot_nn(block, out_time[...])
    after[...] = after_value
    inv_space = lax.rsqrt(jnp.mean(after_value * after_value, axis=-1, keepdims=True) + epsilon)
    sums = add([base[:, low:high] for low, high in cuts], project(block, fold))
    queries, key_rows, values = by_heads([inv_space * part for part in sums])
    values = jnp.concatenate([values, jnp.zeros((tokens, extra), jnp.bfloat16)], axis=1)
    parts = []
    for group in whole_group:
        probs = probabilities(queries, key_rows, bias_turned, group)
        parts.append(back(queries, key_rows, dc_space, values, probs, group))
    after_ctx = dot_nn(after[...].astype(jnp.bfloat16), out_time_t[...])
    grads = grads_of(parts)
    stack_grads(*grads)
    lean = weighted_sum(grads, (queries, key_rows, values)) * (inv_space * inv_space / width)
    rest_ctx = cot_ctx - lean * after_ctx
    dc_move = exchange(chunk_count + 1, send_dc, got_dc, 0, wide)
    grad_ctx = rest_ctx + inv_space * dot_nn(stacked[...], fold_t[...])
    lane = lax.broadcasted_iota(jnp.int32, (1, wide), 1)
    high = inv_time.astype(jnp.bfloat16).astype(jnp.float32)
    spare = jnp.where(lane < HEADS * HD + extra // 2, high, inv_time - high)
    send_dc[...] = split(jnp.where(lane < HEADS * HD, grad_ctx, spare))
    dc_move[0]()
    turn(proj_space, proj_space_t)
    grad_normed = dot_nn(stacked[...], proj_space_t[...])
    grad_after = (
        cot_ref[...].astype(jnp.float32) + inv_space * (grad_normed * gain) - lean * after[...]
    )
    after[...] = grad_after
    after_send[...] = after[pl.ds(pl.multiple_of(other * half, half), half), :].astype(jnp.bfloat16)

    def pair_copy(place, source, target):
        return pltpu.make_async_remote_copy(
            src_ref=source,
            dst_ref=target,
            send_sem=pair_send_sems.at[place],
            recv_sem=pair_recv_sems.at[place],
            device_id=(me, other),
            device_id_type=pl.DeviceIdType.MESH,
        )

    after_copy = pair_copy(0, after_send, after_got)
    after_copy.start()

    turn(proj_time, proj_time_t)
    dc_move[1]()
    block = merged(got_dc)
    inv_rows = block[:, HEADS * HD : HEADS * HD + 1] + block[:, wide - 1 :]
    dc_time[...] = block.astype(jnp.bfloat16)
    parts = []
    for group in whole_group:
        probs = [probs_time[pair] for pair in group]
        parts.append(back(q_time, k_time, dc_time, v_time, probs, group))
    grads = grads_of(parts)
    stack_grads(*grads)
    lean = weighted_sum(grads, (q_time, k_time, v_time)) * (1.0 / width)
    gain = gain_row(gain_time_ref)
    inverse = 1.0 / gain
    tilt = merged(got_normed) * inverse * lean
    total = inv_rows * (dot_nn(stacked[...], proj_time_t[...]) * gain - tilt)
    total = total + pltpu.roll(total, tokens - share_rows, 0)
    send_back[...] = split(total)
    my_slot = lax.rem(me, half_blocks)
    my_half = me // half_blocks
    send_sem, recv_sem = back_sems.at[0], back_sems.at[1]

    def back_copy(target):
        return pltpu.make_async_remote_copy(
            src_ref=send_back.at[target, pl.ds(0, share_rows)],
            dst_ref=got_back.at[my_slot, share(core)],
            send_sem=send_sem,
            recv_sem=recv_sem,
            device_id=(target, my_half),
            device_id_type=pl.DeviceIdType.MESH,
        )

    for step in range(seq_count - 1, 0, -1):
        back_copy(partner(step)).start()

    @pl.when(my_half != core)
    def _():
        back_copy(me).start()

    @pl.when(my_half == core)
    def _():
        source = send_back.at[me, pl.ds(0, share_rows)]
        stay(source, got_back.at[my_slot, share(core)], send_sem, recv_sem, phases)

    whole_back = pltpu.make_async_remote_copy(
        src_ref=send_back.at[pl.ds(0, half_blocks)],
        dst_ref=got_back,
        send_sem=send_sem,
        recv_sem=recv_sem,
        device_id=(me, other),
        device_id_type=pl.DeviceIdType.MESH,
    )
    after_copy.wait_recv()
    kept = after[pl.ds(pl.multiple_of(core * half, half), half), :]
    out_ref[...] = kept + after_got[...].astype(jnp.float32)
    whole_back.wait_recv()
    out_ref[...] += got_back[...].astype(jnp.float32).reshape(half, width)
    whole_back.wait_send()
    for _, _, finish in (*normed_moves, ctx_move, dc_move):
        finish()
    for copy in (*pair_copies, after_copy):
        copy.wait_send()


def fused_device(
    clip,
    offsets,
    cotangent,
    gain_time,
    gain_space,
    proj_time,
    out_time,
    proj_space,
    out_space,
    bias_time,
    bias_space,
):
    seq_count = lax.axis_size("seq")
    tokens, width = clip.shape[1:]
    rows = tokens // seq_count
    head_cols = HEADS * HD
    wide = -(-head_cols // LANES) * LANES
    half, half_blocks = tokens // 2, seq_count // 2
    moves = 3
    f32, bf16 = jnp.float32, jnp.bfloat16
    vmem = pltpu.VMEM
    dma = pltpu.SemaphoreType.DMA
    scratch = [
        vmem((tokens, width), bf16),
        vmem((tokens, width), bf16),
        vmem((tokens, width), bf16),
        vmem((width // LANES, LANES), f32),
        vmem((width // LANES, LANES), f32),
        vmem((HEADS * seq_count, seq_count), f32),
        vmem((3 * head_cols, width), bf16),
        vmem((width, wide), bf16),
        vmem((3 * head_cols, width), bf16),
        vmem((width, 3 * head_cols), bf16),
        vmem((wide, width), bf16),
        vmem((width, 3 * head_cols), bf16),
        vmem((wide, width), bf16),
        vmem((HEADS, tokens, tokens), f32),
        vmem((HEADS // 2, 2 * tokens, tokens), f32),
        vmem((HEADS // 2, 2 * tokens, tokens), f32),
        vmem((wide + tokens, width), bf16),
        vmem((wide, 3 * head_cols), bf16),
        vmem((3 * head_cols, wide), bf16),
        vmem((tokens, 3 * head_cols), f32),
        vmem((tokens, width), f32),
        vmem((tokens, width), f32),
        vmem((tokens, wide), bf16),
        vmem((tokens, wide), bf16),
        vmem((tokens, wide), bf16),
        vmem((HEADS // 2, 2 * tokens, tokens), f32),
        vmem((tokens, 3 * head_cols), bf16),
        vmem((tokens, wide), bf16),
        vmem((tokens, wide), bf16),
        vmem((seq_count, rows, width), bf16),
        vmem((seq_count, rows, width), bf16),
        vmem((seq_count, rows, wide), bf16),
        vmem((seq_count, rows, wide), bf16),
        vmem((seq_count, rows, wide), bf16),
        vmem((seq_count, rows, wide), bf16),
        vmem((moves + 1, rows, width), bf16),
        vmem((seq_count, rows, width), bf16),
        vmem((half_blocks, rows, width), bf16),
        vmem((half, width), bf16),
        vmem((half, width), bf16),
        dma((moves,)),
        dma((moves,)),
        dma((2,)),
        dma((5,)),
        dma((5,)),
        dma((5,)),
        dma((1,)),
        dma((1,)),
        dma((6,)),
    ]
    out_vmem = pl.BlockSpec(memory_space=pltpu.VMEM)
    anywhere = pl.BlockSpec(memory_space=pl.ANY)
    out = pl.pallas_call(
        functools.partial(fused_kernel, seq_count),
        out_shape=pltpu.VMEM((half, width), f32),
        in_specs=[anywhere] * 11,
        out_specs=out_vmem,
        scratch_shapes=scratch,
        compiler_params=pltpu.CompilerParams(
            collective_id=0, has_side_effects=True, vmem_limit_bytes=56 * 1024 * 1024
        ),
    )(
        clip[0],
        offsets[0, 0],
        cotangent[0, 0],
        gain_time.reshape(-1, LANES),
        gain_space.reshape(-1, LANES),
        bias_time.reshape(HEADS * bias_time.shape[1], bias_time.shape[2]),
        proj_time,
        out_time,
        proj_space,
        out_space,
        bias_space,
    )
    return out[None]


def on_device(clip, *rest):
    seq_count = lax.axis_size("seq")
    tokens = clip.shape[1]
    fits = (
        lax.axis_size("dp") == 2
        and clip.shape[0] == 1
        and seq_count & (seq_count - 1) == 0
        and tokens == 8 * seq_count
        and tokens == LANES
        and clip.shape[2] % LANES == 0
    )
    return (fused_device if fits else per_device)(clip, *rest)


def solution(mesh):
    in_specs = (
        P("seq", None, None),
        P("dp", "seq", None, None),
        P("dp", "seq", None, None),
        P(),
        P(),
        P("dp", None),
        P("dp", None),
        P("dp", None),
        P("dp", None),
        P(),
        P(None, "dp", None),
    )
    out_specs = P("seq", "dp", None)
    return jax.shard_map(
        on_device, mesh=mesh, in_specs=in_specs, out_specs=out_specs, check_vma=False
    )
```

```python
import functools
import math

import jax
import jax.numpy as jnp
from jax import lax
from jax.experimental import pallas as pl
from jax.experimental.pallas import tpu as pltpu
from jax.sharding import PartitionSpec as P

HEADS = 8
HD = 72


epsilon = 1e-06


def rms_norm(hidden_in, gain_vec):
    inv_rms = lax.rsqrt(jnp.mean(hidden_in * hidden_in, axis=-1, keepdims=True) + epsilon)
    return ((hidden_in * inv_rms * gain_vec).astype(jnp.bfloat16), inv_rms)


def norm_back(hidden_in, inv_rms, gain_vec, grad_normed):
    weighted = grad_normed.astype(jnp.float32) * gain_vec
    cubed = inv_rms * inv_rms * inv_rms
    return inv_rms * weighted - hidden_in * cubed * jnp.mean(
        weighted * hidden_in, axis=-1, keepdims=True
    )


def layout_forms(frame_major):
    if frame_major:
        return ("lbhe", "mbhe")
    return ("blhe", "bmhe")


def attend(queries, key_rows, values, score_bias, frame_major):
    query_form, key_form = layout_forms(frame_major)
    scaling = 1.0 / math.sqrt(queries.shape[-1])
    scores = (
        jnp.einsum(
            query_form + "," + key_form + "->bhlm",
            queries,
            key_rows,
            preferred_element_type=jnp.float32,
        )
        * scaling
        + score_bias
    )
    highest = jnp.max(scores, axis=-1, keepdims=True)
    exp_scores = jnp.exp(scores - highest)
    probabilities = exp_scores / jnp.sum(exp_scores, axis=-1, keepdims=True)
    context = jnp.einsum(
        "bhlm," + key_form + "->" + query_form,
        probabilities.astype(jnp.bfloat16),
        values,
        preferred_element_type=jnp.float32,
    )
    return (context.astype(jnp.bfloat16), probabilities)


def attend_back(queries, key_rows, values, probabilities, grad_context, frame_major):
    query_form, key_form = layout_forms(frame_major)
    scaling = 1.0 / math.sqrt(queries.shape[-1])
    rounded = probabilities.astype(jnp.bfloat16)
    grad_values = jnp.einsum(
        "bhlm," + query_form + "->" + key_form,
        rounded,
        grad_context,
        preferred_element_type=jnp.float32,
    ).astype(jnp.bfloat16)
    grad_probs = jnp.einsum(
        query_form + "," + key_form + "->bhlm",
        grad_context,
        values,
        preferred_element_type=jnp.float32,
    )
    row_sums = jnp.sum(grad_probs * probabilities, axis=-1, keepdims=True)
    grad_scores = (probabilities * (grad_probs - row_sums) * scaling).astype(jnp.bfloat16)
    grad_queries = jnp.einsum(
        "bhlm," + key_form + "->" + query_form,
        grad_scores,
        key_rows,
        preferred_element_type=jnp.float32,
    ).astype(jnp.bfloat16)
    grad_keys = jnp.einsum(
        "bhlm," + query_form + "->" + key_form,
        grad_scores,
        queries,
        preferred_element_type=jnp.float32,
    ).astype(jnp.bfloat16)
    return (grad_queries, grad_keys, grad_values)


def times_transposed(left, weight):
    return lax.dot_general(
        left, weight, (((1,), (1,)), ((), ())), preferred_element_type=jnp.float32
    )


def regroup(arranged):
    return lax.all_to_all(arranged, "seq", split_axis=0, concat_axis=1, tiled=True)


def to_positions(matrix, stack_count):
    seq_count = lax.axis_size("seq")
    local_rows = matrix.shape[0] // seq_count
    col_count = matrix.shape[1] // stack_count
    arranged = matrix.reshape(seq_count, 1, local_rows, stack_count, col_count)
    return regroup(arranged)[0]


def to_frames(arranged):
    seq_count = lax.axis_size("seq")
    frame_count, local_rows, stack_count, col_count = arranged.shape
    returned = regroup(arranged.reshape(frame_count, 1, local_rows, stack_count, col_count))
    return returned.reshape(seq_count * local_rows, stack_count * col_count)


def per_device(
    clip,
    offsets,
    cotangent,
    gain_time,
    gain_space,
    proj_time,
    out_time,
    proj_space,
    out_space,
    bias_time,
    bias_space,
):
    proj_time, out_time, proj_space, out_space = (
        lax.all_gather(proj_time, "dp", axis=0, tiled=True),
        lax.all_gather(out_time, "dp", axis=0, tiled=True),
        lax.all_gather(proj_space, "dp", axis=0, tiled=True),
        lax.all_gather(out_space, "dp", axis=0, tiled=True),
    )
    bias_space = lax.all_gather(bias_space, "dp", axis=1, tiled=True)
    seq_count = lax.axis_size("seq")
    pos_count = clip.shape[1]
    local_rows = pos_count // seq_count
    head_cols = HEADS * HD
    hidden_in = clip[0].astype(jnp.float32) + offsets[0, 0].astype(jnp.float32)
    normed, inv_rms = rms_norm(hidden_in, gain_time)
    arranged_in = to_positions(normed, 1)
    flat_in = arranged_in.reshape(seq_count * local_rows, arranged_in.shape[-1])
    arranged = jnp.dot(flat_in, proj_time, preferred_element_type=jnp.float32).astype(jnp.bfloat16)
    arranged = arranged.reshape(seq_count, local_rows, 3, HEADS, HD)
    queries, key_rows, values = (arranged[:, :, 0], arranged[:, :, 1], arranged[:, :, 2])
    context, weights_time = attend(queries, key_rows, values, bias_time, True)
    context_frames = to_frames(context.reshape(seq_count, local_rows, 1, head_cols))
    after_time = hidden_in + jnp.dot(context_frames, out_time, preferred_element_type=jnp.float32)
    normed_space, inv_rms_space = rms_norm(after_time, gain_space)
    stacked_space = jnp.dot(normed_space, proj_space, preferred_element_type=jnp.float32).astype(
        jnp.bfloat16
    )
    stacked_space = stacked_space.reshape(1, pos_count, 3, HEADS, HD)
    queries_space, keys_space, values_space = (
        stacked_space[:, :, 0],
        stacked_space[:, :, 1],
        stacked_space[:, :, 2],
    )
    unused_context, weights_space = attend(
        queries_space, keys_space, values_space, bias_space, False
    )
    grad_out = cotangent[0, 0]
    grad_context = (
        times_transposed(grad_out, out_space).astype(jnp.bfloat16).reshape(1, pos_count, HEADS, HD)
    )
    grads_space = attend_back(
        queries_space, keys_space, values_space, weights_space, grad_context, False
    )
    grad_normed = times_transposed(
        jnp.stack(grads_space, axis=2).reshape(pos_count, 3 * head_cols), proj_space
    ).astype(jnp.bfloat16)
    grad_after = grad_out.astype(jnp.float32) + norm_back(
        after_time, inv_rms_space, gain_space, grad_normed
    )
    grad_context_time = times_transposed(grad_after.astype(jnp.bfloat16), out_time).astype(
        jnp.bfloat16
    )
    grad_context_pos = to_positions(grad_context_time, 1).reshape(seq_count, local_rows, HEADS, HD)
    grads_time = attend_back(queries, key_rows, values, weights_time, grad_context_pos, True)
    stacked_grads = jnp.stack(grads_time, axis=2)
    grad_pos = times_transposed(
        stacked_grads.reshape(seq_count * local_rows, 3 * head_cols), proj_time
    ).astype(jnp.bfloat16)
    grad_normed_time = to_frames(grad_pos.reshape(seq_count, local_rows, 1, grad_pos.shape[-1]))
    grad_in = grad_after + norm_back(hidden_in, inv_rms, gain_time, grad_normed_time)
    summed = lax.psum_scatter(
        grad_in.astype(jnp.bfloat16), "dp", scatter_dimension=0, tiled=True
    ).astype(jnp.float32)
    return summed[None]


LANES = 128
MASKED = -1e30


def dot_nn(left, right):
    return lax.dot_general(left, right, (((1,), (0,)), ((), ())), preferred_element_type=jnp.float32)


def dot_nt(left, right):
    return lax.dot_general(left, right, (((1,), (1,)), ((), ())), preferred_element_type=jnp.float32)


def dot_tn(left, right):
    return lax.dot_general(left, right, (((0,), (0,)), ((), ())), preferred_element_type=jnp.float32)


def pair_window(pair):
    first = 2 * pair * HD // LANES * LANES
    last = -(-2 * (pair + 1) * HD // LANES) * LANES
    return first, last


def head_lanes(head, first, last):
    lane = lax.broadcasted_iota(jnp.int32, (1, last - first), 1) + first
    return (lane >= head * HD) & (lane < (head + 1) * HD)


def two_heads(block, pair):
    first, last = pair_window(pair)
    piece = block[:, first:last]
    rows = [
        jnp.where(head_lanes(head, first, last), piece, jnp.zeros_like(piece))
        for head in (2 * pair, 2 * pair + 1)
    ]
    return jnp.concatenate(rows, axis=0)


def add_tiles(tiles, first, block):
    for col in range(0, block.shape[1], LANES):
        tile = (first + col) // LANES
        piece = block[:, col : col + LANES]
        tiles[tile] = piece if tiles[tile] is None else tiles[tile] + piece


def pick_tiles(blocks, tokens, tile_count):
    tiles = []
    for tile in range(tile_count):
        low, high = tile * LANES, (tile + 1) * LANES
        value = jnp.zeros((tokens, LANES), jnp.float32)
        for head in range(HEADS):
            if head * HD < high and (head + 1) * HD > low:
                first, _ = pair_window(head // 2)
                row = head % 2 * tokens
                piece = blocks[head // 2][row : row + tokens, low - first : high - first]
                value = jnp.where(head_lanes(head, low, high), piece, value)
        tiles.append(value)
    return tiles


def softmax_keys(scores, tokens):
    halves = []
    for row in range(0, scores.shape[0], tokens):
        block = scores[row : row + tokens]
        exp_block = jnp.exp(block - jnp.max(block, axis=0, keepdims=True))
        halves.append(exp_block * (1.0 / jnp.sum(exp_block, axis=0, keepdims=True)))
    return jnp.concatenate(halves, axis=0)


def score_grads(grad_probs, probs, tokens, scaling):
    halves = []
    for row in range(0, probs.shape[0], tokens):
        weights, grads = probs[row : row + tokens], grad_probs[row : row + tokens]
        mean = jnp.sum(grads * weights, axis=0, keepdims=True)
        halves.append((weights * (grads - mean) * scaling).astype(jnp.bfloat16))
    return jnp.concatenate(halves, axis=0)


def fused_kernel(
    seq_count,
    clip_in,
    off_in,
    cot_in,
    gain_time_in,
    gain_space_in,
    bias_time_in,
    proj_time_in,
    out_time_in,
    proj_space_in,
    out_space_in,
    bias_space_in,
    out_ref,
    clip_ref,
    off_ref,
    cot_ref,
    gain_time_ref,
    gain_space_ref,
    bias_time_ref,
    proj_time_t,
    out_time_t,
    proj_space_t,
    proj_time,
    out_time,
    proj_space,
    out_space,
    bias_space,
    bias_turned,
    bias_wide,
    fold_in,
    fold,
    fold_t,
    base,
    hidden,
    after,
    q_time,
    k_time,
    v_time,
    probs_time,
    stacked,
    dc_space,
    dc_time,
    send_normed,
    got_normed,
    send_ctx,
    got_ctx,
    send_dc,
    got_dc,
    spare_rows,
    spare_ctx,
    send_back,
    got_back,
    after_send,
    after_got,
    send_sems,
    recv_sems,
    back_sems,
    weight_sems,
    weight_send_sems,
    pair_send_sems,
    pair_recv_sems,
    input_sems,
):
    me = lax.axis_index("seq")
    core = lax.axis_index("dp")
    other = 1 - core
    tokens, width = hidden.shape
    rows = tokens // seq_count
    half = tokens // 2
    half_blocks = seq_count // 2
    phases = spare_rows.shape[0] - 1
    wide = q_time.shape[1]
    scaling = 1.0 / math.sqrt(HD)

    barrier = pltpu.get_barrier_semaphore()
    for step in range(seq_count):
        peer = lax.rem(me + step, seq_count)
        if step:
            pl.semaphore_signal(
                barrier, inc=1, device_id=(peer, core), device_id_type=pl.DeviceIdType.MESH
            )
        pl.semaphore_signal(
            barrier, inc=1, device_id=(peer, other), device_id_type=pl.DeviceIdType.MESH
        )

    inputs = (clip_in, off_in, gain_time_in, cot_in, bias_time_in, gain_space_in)
    places = (clip_ref, off_ref, gain_time_ref, cot_ref, bias_time_ref, gain_space_ref)
    input_copies = [
        pltpu.make_async_copy(source, target, input_sems.at[place])
        for place, (source, target) in enumerate(zip(inputs, places))
    ]
    for copy in input_copies:
        copy.start()

    sources = (out_space_in, proj_time_in, out_time_in, proj_space_in)
    targets = (out_space, proj_time, out_time, proj_space)

    def part(place):
        if place == len(sources):
            count = bias_space_in.shape[1]
            start = pl.multiple_of(core * count, count)
            return bias_space_in, bias_space.at[:, pl.ds(start, count)]
        count = sources[place].shape[0]
        start = pl.multiple_of(core * count, count)
        return sources[place], targets[place].at[pl.ds(start, count)]

    weight_count = len(sources) + 1
    own_copies, pair_copies = [], []
    for place in range(weight_count):
        source, target = part(place)
        own_copies.append(pltpu.make_async_copy(source, target, weight_sems.at[place]))
        pair_copies.append(
            pltpu.make_async_remote_copy(
                src_ref=source,
                dst_ref=target,
                send_sem=weight_send_sems.at[place],
                recv_sem=weight_sems.at[place],
                device_id=(me, other),
                device_id_type=pl.DeviceIdType.MESH,
            )
        )

    def weight_ready(place):
        if place == len(sources):
            full = bias_space
        else:
            full = targets[place].at[pl.ds(0, 2 * sources[place].shape[0])]
        pltpu.make_async_remote_copy(
            src_ref=full,
            dst_ref=full,
            send_sem=weight_send_sems.at[place],
            recv_sem=weight_sems.at[place],
            device_id=(me, other),
            device_id_type=pl.DeviceIdType.MESH,
        ).wait_recv()

    def partner(step):
        place, bit = me, 1
        while bit <= step:
            if step & bit:
                place = place + bit * (1 - 2 * (me // bit % 2))
            bit *= 2
        return place

    share_rows = rows // 2
    quarter = seq_count // 4
    far = [*range(3 * quarter - 1, 2 * quarter - 1, -1), *range(seq_count - 1, 3 * quarter - 1, -1)]
    steps = [*far, *range(2 * quarter - 1, 0, -1)]

    def share(to):
        return pl.ds(pl.multiple_of(to * share_rows, share_rows), share_rows)

    def stay(source, target, send_sem, recv_sem, phase):
        pltpu.make_async_copy(source, target, recv_sem).start()
        if source.shape[-1] == head_cols:
            unused = spare_ctx.at[pl.ds(0, share_rows)]
        else:
            unused = spare_rows.at[phase, pl.ds(0, share_rows), pl.ds(0, source.shape[-1])]
        pltpu.make_async_copy(source, unused, send_sem).start()

    def exchange(phase, sent, got, first, last):
        columns = slice(None)

        def start():
            for step, to in (*[(step, 1) for step in steps], *[(step, 0) for step in steps], (0, other)):
                target = partner(step)
                pltpu.make_async_remote_copy(
                    src_ref=sent.at[target, share(to), columns],
                    dst_ref=got.at[me, share(core), columns],
                    send_sem=send_sems.at[phase],
                    recv_sem=recv_sems.at[phase],
                    device_id=(target, to),
                    device_id_type=pl.DeviceIdType.MESH,
                ).start()
            own = sent.at[me, share(core), columns]
            stay(own, got.at[me, share(core), columns], send_sems.at[phase], recv_sems.at[phase], phase)

        def whole():
            return pltpu.make_async_remote_copy(
                src_ref=sent.at[:, :, columns],
                dst_ref=got.at[:, :, columns],
                send_sem=send_sems.at[phase],
                recv_sem=recv_sems.at[phase],
                device_id=(me, other),
                device_id_type=pl.DeviceIdType.MESH,
            )

        def arrive():
            whole().wait_recv()

        def finish():
            whole().wait_send()

        return start, arrive, finish

    def merged(ref, first=0, last=None):
        last = ref.shape[-1] if last is None else last
        block = ref[:, :, first:last].astype(jnp.float32)
        return block.reshape(tokens, last - first)

    def split(value):
        return value.reshape(seq_count, rows, value.shape[-1]).astype(jnp.bfloat16)

    def gain_row(gain_ref):
        pieces = [gain_ref[place : place + 1, :] for place in range(gain_ref.shape[0])]
        return jnp.concatenate(pieces, axis=1)

    def norm(value, gain_ref):
        inv_rms = lax.rsqrt(jnp.mean(value * value, axis=-1, keepdims=True) + epsilon)
        return value * inv_rms * gain_row(gain_ref), inv_rms

    head_cols = HEADS * HD
    whole_cols = head_cols // LANES * LANES
    cuts = ((0, whole_cols), (whole_cols, 2 * head_cols), (2 * head_cols, 3 * head_cols))

    def project(block, weight):
        return [dot_nn(block, weight[:, low:high]) for low, high in cuts]

    def add(sums, terms):
        return [a + b for a, b in zip(sums, terms)]

    def by_heads(sums):
        left, middle, values = sums
        queries = jnp.concatenate([left, middle[:, :LANES]], axis=1)
        key_rows = pltpu.roll(middle, middle.shape[1] - (head_cols - whole_cols), 1)
        return queries.astype(jnp.bfloat16), key_rows.astype(jnp.bfloat16), values.astype(jnp.bfloat16)

    def weighted_sum(grads, stacks):
        total = None
        for tiles, stack in zip(grads, stacks):
            for tile, value in enumerate(tiles):
                term = value * stack[:, tile * LANES : (tile + 1) * LANES].astype(jnp.float32)
                total = term if total is None else total + term
        return jnp.sum(total, axis=-1, keepdims=True)

    def stack_grads(dq, dk, dv):
        whole = whole_cols
        dq = jnp.concatenate(dq, axis=1)
        dk = pltpu.roll(jnp.concatenate(dk, axis=1), head_cols - whole, 1)
        dv = jnp.concatenate(dv, axis=1)
        stacked[:, :whole] = dq[:, :whole].astype(jnp.bfloat16)
        stacked[:, whole : whole + LANES] = (dq[:, whole:] + dk[:, :LANES]).astype(jnp.bfloat16)
        stacked[:, whole + LANES : 2 * head_cols] = dk[:, LANES:].astype(jnp.bfloat16)
        stacked[:, 2 * head_cols :] = dv[:, :head_cols].astype(jnp.bfloat16)

    def back(queries, key_rows, grad_ctx, values, probs, pairs):
        windows = [pair_window(pair) for pair in pairs]
        ctxs = [grad_ctx[:, first:last] for first, last in windows]
        grads = [dot_nt(two_heads(values, pair), ctx) for pair, ctx in zip(pairs, ctxs)]
        dv = [dot_nn(block.astype(jnp.bfloat16), ctx) for block, ctx in zip(probs, ctxs)]
        ds = [score_grads(grad, block, tokens, scaling) for grad, block in zip(grads, probs)]
        dk = [dot_nn(block, queries[:, first:last]) for block, (first, last) in zip(ds, windows)]
        dq = [dot_tn(block, two_heads(key_rows, pair)) for block, pair in zip(ds, pairs)]
        return dq, dk, dv

    def grads_of(parts):
        dq, dk, dv = (sum((part[place] for part in parts), []) for place in range(3))
        tiles = [None] * tile_count
        for pair, block in enumerate(dq):
            add_tiles(tiles, pair_window(pair)[0], block)
        return tiles, pick_tiles(dk, tokens, tile_count), pick_tiles(dv, tokens, tile_count)

    def turn(weight, turned):
        for first in range(0, weight.shape[0], LANES):
            turned[:, first : first + LANES] = weight[first : first + LANES, :].T

    tile_count = wide // LANES

    for copy in input_copies[:3]:
        copy.wait()
    for place in (0, 4, 1, 2, 3):
        own_copies[place].start()
    hidden[...] = clip_ref[...].astype(jnp.float32) + off_ref[...].astype(jnp.float32)
    normed, inv_time = norm(hidden[...], gain_time_ref)
    send_normed[...] = split(normed)
    pl.semaphore_wait(barrier, 2 * seq_count - 1)
    feature_cuts = [0, width]
    chunk_count = len(feature_cuts) - 1
    normed_moves = [
        exchange(place, send_normed, got_normed, feature_cuts[place], feature_cuts[place + 1])
        for place in range(chunk_count)
    ]
    for start, _, _ in normed_moves:
        start()
    for place in (0, 4, 1, 2, 3):
        pair_copies[place].start()

    extra = wide - HEADS * HD
    for ref in (out_time, out_space):
        ref[pl.ds(HEADS * HD, extra), :] = jnp.zeros((extra, width), jnp.bfloat16)
    frame = lax.broadcasted_iota(jnp.int32, (seq_count, tokens), 0)
    column = lax.broadcasted_iota(jnp.int32, (seq_count, tokens), 1)
    spread = jnp.where(column // rows == frame, 1.0, 0.0).astype(jnp.float32)
    same = lax.broadcasted_iota(jnp.int32, (tokens, tokens), 0) % rows == (
        lax.broadcasted_iota(jnp.int32, (tokens, tokens), 1) % rows
    )
    for copy in input_copies[3:]:
        copy.wait()
    for head in range(HEADS):
        block = lax.dot_general(
            bias_time_ref[head * seq_count : (head + 1) * seq_count, :],
            spread,
            (((0,), (0,)), ((), ())),
            precision=lax.Precision.HIGHEST,
            preferred_element_type=jnp.float32,
        )
        block = jnp.broadcast_to(block[:, None, :], (seq_count, rows, tokens))
        row = head % 2 * tokens
        bias_wide[head // 2, row : row + tokens, :] = jnp.where(
            same, block.reshape(tokens, tokens), MASKED
        )

    weight_ready(0)
    dc_space[...] = dot_nt(cot_ref[...], out_space[...]).astype(jnp.bfloat16)

    weight_ready(4)
    for head in range(HEADS):
        row = head % 2 * tokens
        bias_turned[head // 2, row : row + tokens, :] = bias_space[head].T
    weight_ready(1)
    weight_ready(2)
    gain = gain_row(gain_space_ref)
    fold_in[:wide, :] = (out_time[...].astype(jnp.float32) * gain).astype(jnp.bfloat16)
    fold_in[wide:, :] = (hidden[...] * gain).astype(jnp.bfloat16)
    turn(out_time, out_time_t)
    cot_ctx = dot_nn(cot_ref[...], out_time_t[...])

    def arrived(place):
        normed_moves[place][1]()
        return merged(got_normed, feature_cuts[place], feature_cuts[place + 1]).astype(jnp.bfloat16)

    sums = project(arrived(0), proj_time.at[: feature_cuts[1]])
    for place in range(1, chunk_count):
        rows_of = proj_time.at[feature_cuts[place] : feature_cuts[place + 1]]
        sums = add(sums, project(arrived(place), rows_of))
    queries, key_rows, values = by_heads(sums)
    q_time[...] = queries
    k_time[...] = key_rows
    v_time[:, : HEADS * HD] = values
    v_time[:, HEADS * HD :] = jnp.zeros((tokens, extra), jnp.bfloat16)
    ctx = [None] * tile_count
    cut = 2 * LANES
    ctx_move = exchange(chunk_count, send_ctx, got_ctx, 0, head_cols)
    pair_count = HEADS // 2

    def probabilities(queries, key_rows, bias, pairs):
        scores = []
        for pair in pairs:
            first, last = pair_window(pair)
            scores.append(dot_nt(two_heads(key_rows, pair), queries[:, first:last]))
        return [
            softmax_keys(block * scaling + bias[pair], tokens) for pair, block in zip(pairs, scores)
        ]

    groups = [range(place, place + 2) for place in range(0, pair_count, 2)]
    whole_group = [range(pair_count)]
    for group in whole_group:
        probs = probabilities(q_time, k_time, bias_wide, group)
        for pair, block in zip(group, probs):
            probs_time[pair] = block
            add_tiles(
                ctx,
                pair_window(pair)[0],
                dot_tn(block.astype(jnp.bfloat16), two_heads(v_time, pair)),
            )
    send_ctx[...] = split(jnp.concatenate(ctx, axis=1)[:, :head_cols])
    ctx_move[0]()
    weight_ready(3)
    for low, high in cuts:
        block = dot_nn(fold_in[...], proj_space[:, low:high])
        fold[:, low:high] = block[:wide].astype(jnp.bfloat16)
        base[:, low:high] = block[wide:]
    turn(fold, fold_t)
    ctx_move[1]()
    block = merged(got_ctx).astype(jnp.bfloat16)
    after_value = hidden[...] + dot_nn(block, out_time[:head_cols])
    after[...] = after_value
    inv_space = lax.rsqrt(jnp.mean(after_value * after_value, axis=-1, keepdims=True) + epsilon)
    sums = add([base[:, low:high] for low, high in cuts], project(block, fold.at[:head_cols]))
    queries, key_rows, values = by_heads([inv_space * part for part in sums])
    values = jnp.concatenate([values, jnp.zeros((tokens, extra), jnp.bfloat16)], axis=1)
    parts = []
    for group in whole_group:
        probs = probabilities(queries, key_rows, bias_turned, group)
        parts.append(back(queries, key_rows, dc_space, values, probs, group))
    after_ctx = dot_nn(after[...].astype(jnp.bfloat16), out_time_t[...])
    grads = grads_of(parts)
    stack_grads(*grads)
    lean = weighted_sum(grads, (queries, key_rows, values)) * (inv_space * inv_space / width)
    rest_ctx = cot_ctx - lean * after_ctx
    dc_move = exchange(chunk_count + 1, send_dc, got_dc, 0, wide)
    grad_ctx = rest_ctx + inv_space * dot_nn(stacked[...], fold_t[...])
    lane = lax.broadcasted_iota(jnp.int32, (1, wide), 1)
    high = inv_time.astype(jnp.bfloat16).astype(jnp.float32)
    spare = jnp.where(lane < HEADS * HD + extra // 2, high, inv_time - high)
    send_dc[...] = split(jnp.where(lane < HEADS * HD, grad_ctx, spare))
    dc_move[0]()
    turn(proj_space, proj_space_t)
    grad_normed = dot_nn(stacked[...], proj_space_t[...])
    grad_after = (
        cot_ref[...].astype(jnp.float32) + inv_space * (grad_normed * gain) - lean * after[...]
    )
    after[...] = grad_after
    after_send[...] = after[pl.ds(pl.multiple_of(other * half, half), half), :].astype(jnp.bfloat16)

    def pair_copy(place, source, target):
        return pltpu.make_async_remote_copy(
            src_ref=source,
            dst_ref=target,
            send_sem=pair_send_sems.at[place],
            recv_sem=pair_recv_sems.at[place],
            device_id=(me, other),
            device_id_type=pl.DeviceIdType.MESH,
        )

    after_copy = pair_copy(0, after_send, after_got)
    after_copy.start()

    turn(proj_time, proj_time_t)
    dc_move[1]()
    block = merged(got_dc)
    inv_rows = block[:, HEADS * HD : HEADS * HD + 1] + block[:, wide - 1 :]
    dc_time[...] = block.astype(jnp.bfloat16)
    parts = []
    for group in whole_group:
        probs = [probs_time[pair] for pair in group]
        parts.append(back(q_time, k_time, dc_time, v_time, probs, group))
    grads = grads_of(parts)
    stack_grads(*grads)
    lean = weighted_sum(grads, (q_time, k_time, v_time)) * (1.0 / width)
    gain = gain_row(gain_time_ref)
    inverse = 1.0 / gain
    tilt = merged(got_normed) * inverse * lean
    total = inv_rows * (dot_nn(stacked[...], proj_time_t[...]) * gain - tilt)
    total = total + pltpu.roll(total, tokens - share_rows, 0)
    send_back[...] = split(total)
    my_slot = lax.rem(me, half_blocks)
    my_half = me // half_blocks
    send_sem, recv_sem = back_sems.at[0], back_sems.at[1]

    def back_copy(target):
        return pltpu.make_async_remote_copy(
            src_ref=send_back.at[target, pl.ds(0, share_rows)],
            dst_ref=got_back.at[my_slot, share(core)],
            send_sem=send_sem,
            recv_sem=recv_sem,
            device_id=(target, my_half),
            device_id_type=pl.DeviceIdType.MESH,
        )

    for step in range(seq_count - 1, 0, -1):
        back_copy(partner(step)).start()

    @pl.when(my_half != core)
    def _():
        back_copy(me).start()

    @pl.when(my_half == core)
    def _():
        source = send_back.at[me, pl.ds(0, share_rows)]
        stay(source, got_back.at[my_slot, share(core)], send_sem, recv_sem, phases)

    whole_back = pltpu.make_async_remote_copy(
        src_ref=send_back.at[pl.ds(0, half_blocks)],
        dst_ref=got_back,
        send_sem=send_sem,
        recv_sem=recv_sem,
        device_id=(me, other),
        device_id_type=pl.DeviceIdType.MESH,
    )
    after_copy.wait_recv()
    kept = after[pl.ds(pl.multiple_of(core * half, half), half), :]
    out_ref[...] = kept + after_got[...].astype(jnp.float32)
    whole_back.wait_recv()
    out_ref[...] += got_back[...].astype(jnp.float32).reshape(half, width)
    whole_back.wait_send()
    for _, _, finish in (*normed_moves, ctx_move, dc_move):
        finish()
    for copy in (*pair_copies, after_copy):
        copy.wait_send()


def fused_device(
    clip,
    offsets,
    cotangent,
    gain_time,
    gain_space,
    proj_time,
    out_time,
    proj_space,
    out_space,
    bias_time,
    bias_space,
):
    seq_count = lax.axis_size("seq")
    tokens, width = clip.shape[1:]
    rows = tokens // seq_count
    head_cols = HEADS * HD
    wide = -(-head_cols // LANES) * LANES
    half, half_blocks = tokens // 2, seq_count // 2
    moves = 3
    f32, bf16 = jnp.float32, jnp.bfloat16
    vmem = pltpu.VMEM
    dma = pltpu.SemaphoreType.DMA
    scratch = [
        vmem((tokens, width), bf16),
        vmem((tokens, width), bf16),
        vmem((tokens, width), bf16),
        vmem((width // LANES, LANES), f32),
        vmem((width // LANES, LANES), f32),
        vmem((HEADS * seq_count, seq_count), f32),
        vmem((3 * head_cols, width), bf16),
        vmem((width, wide), bf16),
        vmem((3 * head_cols, width), bf16),
        vmem((width, 3 * head_cols), bf16),
        vmem((wide, width), bf16),
        vmem((width, 3 * head_cols), bf16),
        vmem((wide, width), bf16),
        vmem((HEADS, tokens, tokens), f32),
        vmem((HEADS // 2, 2 * tokens, tokens), f32),
        vmem((HEADS // 2, 2 * tokens, tokens), f32),
        vmem((wide + tokens, width), bf16),
        vmem((wide, 3 * head_cols), bf16),
        vmem((3 * head_cols, wide), bf16),
        vmem((tokens, 3 * head_cols), f32),
        vmem((tokens, width), f32),
        vmem((tokens, width), f32),
        vmem((tokens, wide), bf16),
        vmem((tokens, wide), bf16),
        vmem((tokens, wide), bf16),
        vmem((HEADS // 2, 2 * tokens, tokens), f32),
        vmem((tokens, 3 * head_cols), bf16),
        vmem((tokens, wide), bf16),
        vmem((tokens, wide), bf16),
        vmem((seq_count, rows, width), bf16),
        vmem((seq_count, rows, width), bf16),
        vmem((seq_count, rows, head_cols), bf16),
        vmem((seq_count, rows, head_cols), bf16),
        vmem((seq_count, rows, wide), bf16),
        vmem((seq_count, rows, wide), bf16),
        vmem((moves + 1, rows, width), bf16),
        vmem((rows, head_cols), bf16),
        vmem((seq_count, rows, width), bf16),
        vmem((half_blocks, rows, width), bf16),
        vmem((half, width), bf16),
        vmem((half, width), bf16),
        dma((moves,)),
        dma((moves,)),
        dma((2,)),
        dma((5,)),
        dma((5,)),
        dma((1,)),
        dma((1,)),
        dma((6,)),
    ]
    out_vmem = pl.BlockSpec(memory_space=pltpu.VMEM)
    anywhere = pl.BlockSpec(memory_space=pl.ANY)
    out = pl.pallas_call(
        functools.partial(fused_kernel, seq_count),
        out_shape=pltpu.VMEM((half, width), f32),
        in_specs=[anywhere] * 11,
        out_specs=out_vmem,
        scratch_shapes=scratch,
        compiler_params=pltpu.CompilerParams(
            collective_id=0, has_side_effects=True, vmem_limit_bytes=56 * 1024 * 1024
        ),
    )(
        clip[0],
        offsets[0, 0],
        cotangent[0, 0],
        gain_time.reshape(-1, LANES),
        gain_space.reshape(-1, LANES),
        bias_time.reshape(HEADS * bias_time.shape[1], bias_time.shape[2]),
        proj_time,
        out_time,
        proj_space,
        out_space,
        bias_space,
    )
    return out[None]


def on_device(clip, *rest):
    seq_count = lax.axis_size("seq")
    tokens = clip.shape[1]
    fits = (
        lax.axis_size("dp") == 2
        and clip.shape[0] == 1
        and seq_count & (seq_count - 1) == 0
        and tokens == 8 * seq_count
        and tokens == LANES
        and clip.shape[2] % LANES == 0
    )
    return (fused_device if fits else per_device)(clip, *rest)


def solution(mesh):
    in_specs = (
        P("seq", None, None),
        P("dp", "seq", None, None),
        P("dp", "seq", None, None),
        P(),
        P(),
        P("dp", None),
        P("dp", None),
        P("dp", None),
        P("dp", None),
        P(),
        P(None, "dp", None),
    )
    out_specs = P("seq", "dp", None)
    return jax.shard_map(
        on_device, mesh=mesh, in_specs=in_specs, out_specs=out_specs, check_vma=False
    )
```
